256 devices in a mesh: fsdp: 8 (over y, core), expert: 32 (over z, x).
Axes of the slice: x: 4, y: 4, z: 8, core: 2. Of those that a mesh axis runs over, the one named last changes fastest.
Arguments:
- tokens: bfloat16 [4096, 4096], P(('fsdp', 'expert')), may hold values from -18 to 18
- learner_rows: bfloat16 [64, 3, 768, 4096], P(None, None, 'expert', 'fsdp'), may hold values from -0.25 to 0.25, as said below
- exponents: int32 [64, 3, 768, 128], P(None, None, 'expert', 'fsdp'), may hold values from -9 to -5
- expert_ids: int32 [4096, 8], P(('fsdp', 'expert')), may hold values from 0 to 63, all different within a row; in each aligned block of 16 rows (0 to 15, 16 to 31, ...) at most 4 rows name the same one
- route_probs: float32 [4096, 8], P(('fsdp', 'expert')), may hold values from 0.05 to 1
Outputs:
- rollout_elements: bfloat16 [64, 3, 768, 4096], P('expert', None, None, 'fsdp')
- mixed: bfloat16 [4096, 4096], P(('fsdp', 'expert'))
The draws below stay inside these ranges and needn't reach their ends.
Inputs may be any that keep to these rules, and one draw needn't show every extreme that they name: `expert_ids`: each row names 8 different experts. Among the rows of one device no expert is named more than 4 times, a bound that some block reaches. `learner_rows`: each entry is at most 8 times its block's scale 2 ** exponent in magnitude.
All inputs are finite; a program needn't handle non-finite values.
Results may differ from the reference program's by a relative error of at most 0.02.
Values may be sent and summed in bfloat16 or wider, within the bound.
A program may use at most 128 MiB of HBM per device.

```python
import math
import jax
import jax.numpy as jnp
import numpy as np
from jax import lax

D = 4096
FF = 768
TOP = 8
BLOCK = 32
TOK_DEV = 16
E = 64
CAP = 4
TOKENS = 4096
N_FSDP = 8
N_EXPERT = 32


def shared_exponents(key):
    return jax.random.randint(jax.random.fold_in(key, 11), (E, 3, FF, D // BLOCK), -9, -4, dtype=jnp.int32)


def draw_exponents(key, part):
    return shared_exponents(key)


def draw_learner_rows(key, part):
    exps = shared_exponents(key)
    second = jax.random.fold_in(key, 23)
    shape = (E, 3, FF, D)
    factor = jnp.clip(1.6 * jax.random.normal(second, shape, jnp.float32), -8.0, 8.0)
    widened = jnp.repeat(jnp.exp2(exps.astype(jnp.float32)), BLOCK, axis=3)
    return (factor * widened).astype(jnp.bfloat16)


def levels(own_key, dims, cuts, least, high):
    loudness = 1.0
    for axis_at, shards_of in cuts:
        steps = jax.random.uniform(jax.random.fold_in(jax.random.fold_in(own_key, 6), axis_at), (shards_of,), jnp.float32, least / len(cuts), high / len(cuts))
        loudness = loudness * jnp.repeat(jnp.exp(steps), dims[axis_at] // shards_of).reshape((-1,) + (1,) * (len(dims) - 1 - axis_at))
    return loudness


def routed_block(key, own, number, rows, amount, top, reach, slope):
    order = jax.random.permutation(key, amount)
    heavy_load, usual = shares(amount, rows * top, reach, slope, True), shares(amount, rows * top, reach, slope, False)
    places = jnp.arange(amount)

    def named(lengths, offset_by):
        used = int((lengths > 0).sum())
        fixed = max(1, used // 4)
        passed = fixed + (places - fixed + offset_by * (used - fixed)) % max(1, amount - fixed)
        return jnp.zeros((amount,), jnp.int32).at[order[jnp.where(places < fixed, places, passed)]].set(jnp.asarray(lengths, jnp.int32))

    lengths = jnp.where(number % 4 == 0, named(heavy_load, number // 4), named(usual, number - number // 4 - 1))
    mixed = jax.random.permutation(jax.random.fold_in(own, 3), amount)
    giver, receiver = mixed[0:amount // 2 * 2:2], mixed[1:amount // 2 * 2:2]
    slack = jnp.minimum(lengths[giver] - 1, reach - lengths[receiver]) // 2
    slack = jnp.where((giver == order[0]) | (receiver == order[0]) | (lengths[receiver] == 0), 0, jnp.maximum(slack, 0))
    passed = jax.random.randint(jax.random.fold_in(own, 4), (amount // 2,), 0, 1 << 20) % (slack + 1)
    lengths = lengths.at[giver].add(-passed).at[receiver].add(passed)
    members = jnp.searchsorted(jnp.cumsum(lengths), jnp.arange(rows * top), side="right").astype(jnp.int32)
    grid = members.reshape(top, rows).T
    grid = grid[jax.random.permutation(jax.random.fold_in(own, 1), rows)]
    offset_by = jax.random.randint(jax.random.fold_in(own, 2), (rows, 1), 0, top)
    return jnp.take_along_axis(grid, (jnp.arange(top)[None, :] + offset_by) % top, axis=1)


def shares(number_of, total, most, slope, full):
    portions = [(1 << 20) // math.isqrt(standing ** slope) + 1 for standing in range(1, number_of + 1)]
    largest = most if full else min(most, max(-(-total // number_of), total * portions[0] // sum(portions)))
    least = 1 if total - largest >= number_of - 1 else 0
    holding, surplus = [largest] + [least] * (number_of - 1), total - largest - least * (number_of - 1)
    while surplus > 0:
        movable = [i for i in range(1, number_of) if holding[i] < largest] or [i for i in range(1, number_of) if holding[i] < most]
        pool, left = sum([portions[i] for i in movable]), surplus
        for i in movable:
            addition = min(most - holding[i], max(1, left * portions[i] // pool), surplus)
            holding[i] = holding[i] + addition
            surplus = surplus - addition
    return np.array(holding)


def scatter_about(rng, dims, deviation, most, cuts=(), kind=jnp.bfloat16):
    level = levels(rng, dims, cuts, -0.22, 0.18) if cuts else 1.0
    values = jax.random.normal(rng, dims, jnp.float32) * deviation * level
    return jnp.minimum(jnp.maximum(values, -most), most).astype(kind)


def setup_inputs(seed: int = 0) -> dict:
    key_of = jax.random.split(jax.random.key(seed), 6)
    tokens = scatter_about(key_of[0], (TOKENS, D), 3.0, 18.0, ((0, 256),))
    learner_rows = draw_learner_rows(jax.random.fold_in(key_of[5], 71), 0)
    exponents = draw_exponents(jax.random.fold_in(key_of[5], 71), 0)
    expert_ids_keys = jax.random.split(jax.random.fold_in(key_of[3], 1), TOKENS // TOK_DEV)
    expert_ids_turns = jax.random.permutation(jax.random.fold_in(key_of[3], 3), TOKENS // TOK_DEV)
    expert_ids = jax.vmap(lambda own, number: routed_block(jax.random.fold_in(key_of[3], 2), own, number, TOK_DEV, E, TOP, CAP, 2))(expert_ids_keys, expert_ids_turns).reshape((TOKENS, TOP))
    route_probs = jnp.clip(jnp.exp(math.log(1.0) - 2.9957323 * jax.random.uniform(key_of[4], (TOKENS, TOP), jnp.float32) ** levels(key_of[4], (TOKENS, TOP), ((0, 256),), -0.2, 0.2)), 0.05, 1.0)
    return dict(tokens=tokens, learner_rows=learner_rows, exponents=exponents, expert_ids=expert_ids, route_probs=route_probs)


def to_grid(ratio):
    clipped = jnp.clip(ratio.astype(jnp.float32), -6.0, 6.0)
    magnitude = jnp.abs(clipped)
    level = 0.5 * (magnitude > 0.25) + 0.5 * (magnitude >= 0.75) + 0.5 * (magnitude > 1.25) + 0.5 * (magnitude >= 1.75)
    level = level + 1.0 * (magnitude > 2.5) + 1.0 * (magnitude >= 3.5) + 2.0 * (magnitude > 5.0)
    return (jnp.sign(clipped) * level.astype(jnp.float32)).astype(jnp.bfloat16)


def encode(pieces):
    rows_part, exponent = pieces
    widened = jnp.repeat(jnp.exp2(exponent.astype(jnp.float32)).astype(jnp.bfloat16), BLOCK, axis=2)
    return to_grid(rows_part / widened)


def reference(tokens, learner_rows, exponents, expert_ids, route_probs):
    devices = N_FSDP * N_EXPERT
    capacity = 2 * TOK_DEV * TOP // E
    rollout_elements = lax.map(encode, (learner_rows, exponents))
    routes = expert_ids.reshape(devices, TOK_DEV * TOP)
    one_hot = (routes[:, :, None] == jnp.arange(E, dtype=jnp.int32)[None, None, :]).astype(jnp.int32)
    position = jnp.sum((jnp.cumsum(one_hot, axis=1) - one_hot) * one_hot, axis=2)
    slot_index = (jnp.arange(devices, dtype=jnp.int32)[:, None] * capacity + position).astype(jnp.int32)
    token_index = jnp.repeat(jnp.arange(TOKENS, dtype=jnp.int32), TOP)
    route_share = route_probs / jnp.sum(route_probs, axis=1, keepdims=True)
    flat_routes = routes.reshape(-1)
    flat_slots = slot_index.reshape(-1)
    table = jnp.full((E, devices * capacity), TOKENS, dtype=jnp.int32).at[flat_routes, flat_slots].set(token_index)
    weight = jnp.zeros((E, devices * capacity), jnp.float32).at[flat_routes, flat_slots].set(route_share.reshape(-1))
    padded = jnp.concatenate([tokens, jnp.zeros((1, D), jnp.bfloat16)], axis=0)
    slot_total = devices * capacity

    def apply_expert(running, pieces):
        elements, exponent, rows_index, rows_weight = pieces
        widened = jnp.repeat(jnp.exp2(exponent.astype(jnp.float32)).astype(jnp.bfloat16), BLOCK, axis=2)
        weights = elements * widened
        gathered = padded[rows_index]
        blocks = gathered.astype(jnp.float32).reshape(slot_total, N_FSDP, D // N_FSDP)
        paired = weights[0:2].astype(jnp.float32).reshape(2, FF, N_FSDP, D // N_FSDP)
        partial_value = jnp.einsum("rfd,ghfd->gfrh", blocks, paired, precision=lax.Precision.HIGHEST)
        partial_value = lax.optimization_barrier(partial_value.astype(jnp.bfloat16)).astype(jnp.float32)
        summed = jnp.sum(partial_value, axis=1)
        hidden = (jax.nn.silu(summed[0]) * summed[1]).astype(jnp.bfloat16)
        output = jnp.dot(hidden, weights[2], preferred_element_type=jnp.float32).astype(jnp.bfloat16)
        running = running.at[rows_index].add(rows_weight[:, None] * output.astype(jnp.float32), mode="drop")
        return running, None

    mixed, _ = lax.scan(apply_expert, jnp.zeros((TOKENS, D), jnp.float32), (rollout_elements, exponents, table, weight))
    return rollout_elements, mixed.astype(jnp.bfloat16)
```

```python
import functools
import jax
import jax.numpy as jnp
from jax import lax
from jax.experimental import pallas as pl
from jax.experimental.pallas import tpu as pltpu
from jax.sharding import PartitionSpec as P

BLOCK = 32
MESH = pl.DeviceIdType.MESH


def encode_send(rows, inv, scl, out, s_out, buf, enc, ssend, load_sem, send_sem, recv_sem, own_sem, sc_send, sc_recv, sc_own):
    me = lax.axis_index("expert")
    n = 32
    barrier = pltpu.get_barrier_semaphore()

    def load(ph):
        k, p = PHASES[ph]
        return pltpu.make_async_copy(rows.at[:, k, p], buf.at[ph % 2], load_sem.at[ph % 2])

    load(0).start()

    def greet(j, c):
        peer = lax.rem(me + j, n)
        pl.semaphore_signal(barrier, inc=1, device_id={"expert": peer}, device_id_type=MESH)
        return c

    lax.fori_loop(1, n, greet, 0)

    def scale_copy(j):
        peer = lax.rem(me + j, n)
        return pltpu.make_async_remote_copy(
            src_ref=scl.at[peer], dst_ref=s_out.at[me], send_sem=sc_send, recv_sem=sc_recv,
            device_id={"expert": peer}, device_id_type=MESH)

    def elem_copy(ph, j):
        k, p = PHASES[ph]
        peer = lax.rem(me + j, n)
        return pltpu.make_async_remote_copy(
            src_ref=enc.at[ph, peer], dst_ref=out.at[k, p, me], send_sem=send_sem.at[ph], recv_sem=recv_sem.at[ph],
            device_id={"expert": peer}, device_id_type=MESH)

    for ph in range(6):
        k, p = PHASES[ph]
        kp = k * 3 + p
        load(ph).wait()
        if ph + 1 < 6:
            load(ph + 1).start()
        lane = lax.broadcasted_iota(jnp.int32, (128, 512), 0)
        feat = lax.broadcasted_iota(jnp.int32, (128, 512), 1)
        pick = (lane == kp * 16 + feat // BLOCK).astype(jnp.bfloat16)

        def enc_one(o, c):
            wide = jnp.dot(inv[o], pick, preferred_element_type=jnp.float32)
            x = buf[ph % 2, o].astype(jnp.float32) * wide
            x = jnp.minimum(jnp.maximum(x, -6.0), 6.0)
            a = jnp.abs(x)
            magic = jnp.where(a < 2.0, 0.5 * 12582912.0, jnp.where(a < 4.0, 12582912.0, 2.0 * 12582912.0))
            enc[ph, o] = ((x + magic) - magic).astype(jnp.bfloat16)
            return c

        lax.fori_loop(0, n, enc_one, 0)
        if ph == 0:
            pl.semaphore_wait(barrier, n - 1)

            def sc_one(j, c):
                scale_copy(j).start()
                return c

            lax.fori_loop(1, n, sc_one, 0)
            pltpu.make_async_copy(scl.at[me], s_out.at[me], sc_own).start()

        def send_one(j, c):
            elem_copy(ph, j).start()
            return c

        lax.fori_loop(1, n, send_one, 0)
        pltpu.make_async_copy(enc.at[ph, me], out.at[k, p, me], own_sem.at[ph]).start()

    for ph in range(6):
        k, p = PHASES[ph]
        pltpu.make_async_copy(enc.at[ph, me], out.at[k, p, me], own_sem.at[ph]).wait()
        many = pl.ds(0, n - 1)
        pltpu.make_async_copy(enc.at[ph, many], out.at[k, p, many], send_sem.at[ph]).wait()
        pltpu.make_async_copy(enc.at[ph, many], out.at[k, p, many], recv_sem.at[ph]).wait()
    pltpu.make_async_copy(scl.at[me], s_out.at[me], sc_own).wait()
    many = pl.ds(0, n - 1)
    pltpu.make_async_copy(scl.at[many], s_out.at[many], sc_send).wait()
    pltpu.make_async_copy(scl.at[many], s_out.at[many], sc_recv).wait()


PHASES = [(0, 0), (0, 1), (1, 0), (1, 1), (0, 2), (1, 2)]


def dispatch(rows, inv, scl):
    vm = pl.BlockSpec(memory_space=pltpu.VMEM)
    hbm = pl.BlockSpec(memory_space=pl.ANY)
    return pl.pallas_call(
        encode_send,
        out_shape=(jax.ShapeDtypeStruct((2, 3, 32, 24, 512), jnp.bfloat16), jax.ShapeDtypeStruct((32, 24, 128), jnp.bfloat16)),
        in_specs=[hbm, vm, hbm],
        out_specs=(hbm, hbm),
        scratch_shapes=[
            pltpu.VMEM((2, 32, 24, 512), jnp.bfloat16),
            pltpu.VMEM((6, 32, 24, 512), jnp.bfloat16),
            pltpu.VMEM((8, 128), jnp.bfloat16),
            pltpu.SemaphoreType.DMA((2,)),
            pltpu.SemaphoreType.DMA((6,)),
            pltpu.SemaphoreType.DMA((6,)),
            pltpu.SemaphoreType.DMA((6,)),
            pltpu.SemaphoreType.DMA,
            pltpu.SemaphoreType.DMA,
            pltpu.SemaphoreType.DMA,
        ],
        compiler_params=pltpu.CompilerParams(collective_id=1, has_side_effects=True, vmem_limit_bytes=40 << 20),
        cost_estimate=pl.CostEstimate(flops=2 * 4608 * 128 * 512, bytes_accessed=14 << 20, transcendentals=0),
        name="encode_send",
    )(rows, inv, scl)


def body(tokens, learner_rows, exponents, expert_ids, route_probs):
    exps = exponents.reshape(32, 2, 3, 24, 16).transpose(0, 3, 1, 2, 4).reshape(32, 24, 96).astype(jnp.float32)
    pad = ((0, 0), (0, 0), (0, 32))
    scl = jnp.pad(jnp.exp2(exps), pad).astype(jnp.bfloat16)
    inv = jnp.pad(jnp.exp2(-exps), pad).astype(jnp.bfloat16)
    el, sc = dispatch(learner_rows.reshape(32, 2, 3, 24, 512), inv, scl)
    elements = el.reshape(2, 3, 768, 512)
    spread = lax.all_to_all(tokens.reshape(16, 8, 512), "fsdp", split_axis=1, concat_axis=0, tiled=True).reshape(128, 512)
    held = lax.all_gather(spread, "expert", axis=0, tiled=True)
    meta = jnp.concatenate([expert_ids.astype(jnp.float32).T, route_probs.T], axis=0)
    meta = lax.all_gather(meta, "fsdp", axis=1, tiled=True)
    meta = lax.all_gather(meta, "expert", axis=0, tiled=False)
    ids = meta[:, :8].astype(jnp.int32)
    probs = meta[:, 8:]
    share = probs / jnp.sum(probs, axis=1, keepdims=True)
    mine = lax.axis_index("expert") * 2 + jnp.arange(2, dtype=jnp.int32)
    hit = (ids[:, None] == mine[None, :, None, None])
    member = jnp.any(hit, axis=2)
    weight = jnp.sum(jnp.where(hit, share[:, None], 0.0), axis=2)
    lane = jnp.arange(128, dtype=jnp.int32)
    tri = ((lane[:, None] // 16 == lane[None, :] // 16) & (lane[:, None] < lane[None, :])).astype(jnp.float32)
    pos = jnp.einsum("gkt,tu->gku", member.astype(jnp.float32), tri).astype(jnp.int32)
    code = jnp.where(member, (lane // 16) * 4 + pos, -1)
    onehot = code[:, :, None, :] == jnp.arange(32, dtype=jnp.int32)[None, None, :, None]
    slots = jnp.einsum("gkst,gtd->kgsd", onehot.astype(jnp.bfloat16), held.reshape(32, 128, 512), preferred_element_type=jnp.float32).astype(jnp.bfloat16).reshape(2, 1024, 512)
    sc = sc.reshape(768, 128)
    scw = jnp.stack([jnp.repeat(sc[:, i * 16:(i + 1) * 16], BLOCK, axis=1) for i in range(6)]).reshape(2, 3, 768, 512)
    weights = elements * scw
    part = jnp.einsum("ksd,kghd->ksgh", slots, weights[:, 0:2], preferred_element_type=jnp.float32).astype(jnp.bfloat16)
    summed = lax.psum_scatter(part, "fsdp", scatter_dimension=1, tiled=True).astype(jnp.float32)
    hidden = (jax.nn.silu(summed[:, :, 0]) * summed[:, :, 1]).astype(jnp.bfloat16)
    hidden = lax.all_gather(hidden, "fsdp", axis=1, tiled=True)
    outs = jnp.einsum("ksh,khd->ksd", hidden, weights[:, 2], preferred_element_type=jnp.float32).astype(jnp.bfloat16)
    blend = onehot.astype(jnp.float32) * weight[:, :, None, :]
    outs_g = outs.reshape(2, 32, 32, 512).transpose(1, 0, 2, 3).reshape(32, 64, 512)
    hi = blend.astype(jnp.bfloat16)
    lo = (blend - hi.astype(jnp.float32)).astype(jnp.bfloat16)
    two = jnp.concatenate([hi.reshape(32, 64, 128), lo.reshape(32, 64, 128)], axis=1)
    mixed = jnp.einsum("gst,gsd->gtd", two, jnp.concatenate([outs_g, outs_g], axis=1), preferred_element_type=jnp.float32)
    mixed = mixed.astype(jnp.bfloat16)
    mine_mixed = lax.psum_scatter(mixed.reshape(4096, 512), "expert", scatter_dimension=0, tiled=True)
    mixed_out = lax.all_to_all(mine_mixed, "fsdp", split_axis=0, concat_axis=1, tiled=True)
    return elements, mixed_out


def solution(mesh):
    return jax.shard_map(
        body,
        mesh=mesh,
        in_specs=(
            P(("fsdp", "expert"), None),
            P(None, None, "expert", "fsdp"),
            P(None, None, "expert", "fsdp"),
            P(("fsdp", "expert"), None),
            P(("fsdp", "expert"), None),
        ),
        out_specs=(P("expert", None, None, "fsdp"), P(("fsdp", "expert"), None)),
        check_vma=False,
    )
```

```python
import functools
import jax
import jax.numpy as jnp
from jax import lax
from jax.experimental import pallas as pl
from jax.experimental.pallas import tpu as pltpu
from jax.sharding import PartitionSpec as P

BLOCK = 32
CAP = 4
TOK = 16
MESH = pl.DeviceIdType.MESH
BF, F32 = jnp.bfloat16, jnp.float32
PHASES = ((0, 0), (0, 1), (1, 0), (1, 1), (0, 2), (1, 2))


def loop(low, high, step):
    def one(i, c):
        step(i)
        return c

    lax.fori_loop(low, high, one, 0)


def layer(dims, rows, inv, scl, tok, meta, out, mixed,
          enc, got, s_in, s_flat, xcol, m_all, m_send, m_col, sbuf, slots, wgu, wdn,
          pa, pb, ra, rb, rc, hid, osend, orecv, pm, pr, fin,
          load_sem, e_send, e_recv, e_own, e_out, sc_sem, t_sem, m_sem, z_sem, zm_sem, x_sem,
          a_sem, b_sem, h_sem, i_sem, o_sem, p_sem, q_sem):
    nz, nx, ny, fs, unit = dims
    ne, nf = nz * nx, 2 * ny
    nb = fs // BLOCK
    gt, gs = nf * TOK, nf * CAP
    half = nz * gs // 2
    hidden = ne * unit
    ex, f = lax.axis_index("expert"), lax.axis_index("fsdp")
    z, x = ex // nx, lax.rem(ex, nx)
    y, core = f // 2, lax.rem(f, 2)
    mate = y * 2 + (1 - core)
    barrier = pltpu.get_barrier_semaphore()

    def to_expert(src, dst, send, recv, e):
        return pltpu.make_async_remote_copy(src_ref=src, dst_ref=dst, send_sem=send, recv_sem=recv,
                                            device_id={"expert": e}, device_id_type=MESH)

    def to_fsdp(src, dst, send, recv, g):
        return pltpu.make_async_remote_copy(src_ref=src, dst_ref=dst, send_sem=send, recv_sem=recv,
                                            device_id={"fsdp": g}, device_id_type=MESH)

    def local(src, dst, sem):
        return pltpu.make_async_copy(src, dst, sem)

    for ph, (k, p) in enumerate(PHASES):
        local(rows.at[:, k, p], enc.at[ph], load_sem.at[ph]).start()

    def greet_expert(j):
        pl.semaphore_signal(barrier, inc=1, device_id={"expert": lax.rem(ex + j, ne)}, device_id_type=MESH)

    def greet_fsdp(j):
        pl.semaphore_signal(barrier, inc=1, device_id={"fsdp": lax.rem(f + j, nf)}, device_id_type=MESH)

    loop(1, nf, greet_fsdp)
    loop(1, ne, greet_expert)
    pl.semaphore_wait(barrier, ne + nf - 2)

    def tok_send(j):
        g = lax.rem(f + j, nf)
        here = pl.ds(pl.multiple_of(f * TOK, TOK), TOK)
        to_fsdp(tok.at[:, pl.ds(pl.multiple_of(g * fs, fs), fs)], xcol.at[z, here], t_sem.at[0], t_sem.at[1], g).start()
        to_fsdp(meta, m_all.at[here], m_sem.at[0], m_sem.at[1], g).start()

    here = pl.ds(pl.multiple_of(f * TOK, TOK), TOK)
    loop(1, nf, tok_send)
    local(tok.at[:, pl.ds(pl.multiple_of(f * fs, fs), fs)], xcol.at[z, here], t_sem.at[2]).start()
    local(meta, m_all.at[here], m_sem.at[2]).start()

    def pick(ph):
        k, p = PHASES[ph]
        lane = lax.broadcasted_iota(jnp.int32, (128, fs), 0)
        feat = lax.broadcasted_iota(jnp.int32, (128, fs), 1)
        return (lane == (k * 3 + p) * nb + feat // BLOCK).astype(BF)

    per = min(8, ne)

    def encode(ph):
        local(rows.at[:, 0, 0], enc.at[ph], load_sem.at[ph]).wait()
        sel = pick(ph)

        def step(i):
            wide = jnp.dot(inv[pl.ds(pl.multiple_of(i * per * unit, per * unit), per * unit), :], sel, preferred_element_type=F32)
            for u in range(per):
                v = enc[ph, i * per + u].astype(F32) * wide[u * unit:(u + 1) * unit]
                v = jnp.minimum(jnp.maximum(v, -6.0), 6.0)
                a = jnp.abs(v)
                magic = jnp.where(a < 2.0, 6291456.0, jnp.where(a < 4.0, 12582912.0, 25165824.0))
                enc[ph, i * per + u] = ((v + magic) - magic).astype(BF)

        loop(0, ne // per, step)

    def zigzag(i):
        return lax.rem(ex + jnp.where(lax.rem(i, 2) == 1, (i + 1) // 2, ne - i // 2), ne)

    def elements_send(ph):
        def step(i):
            e = zigzag(i)
            to_expert(enc.at[ph, e], got.at[ph, ex], e_send.at[ph], e_recv.at[ph], e).start()

        loop(1, ne, step)
        local(enc.at[ph, ex], got.at[ph, ex], e_own.at[ph]).start()

    def scales_send(i):
        e = zigzag(i)
        to_expert(scl.at[e], s_in.at[ex], sc_sem.at[0], sc_sem.at[1], e).start()

    encode(0)

    many_f = pl.ds(0, (nf - 1) * TOK)
    local(xcol.at[z, many_f], xcol.at[z, many_f], t_sem.at[1]).wait()
    local(xcol.at[z, here], xcol.at[z, here], t_sem.at[2]).wait()
    local(m_all.at[many_f], m_all.at[many_f], m_sem.at[1]).wait()
    local(meta, m_all.at[here], m_sem.at[2]).wait()
    turned = jnp.transpose(m_all[...])
    m_send[...] = turned.reshape(128 // 16, 16, gt)[:nz]

    def z_send(j):
        to = lax.rem(z + j, nz)
        to_expert(xcol.at[z], xcol.at[z], z_sem.at[0], z_sem.at[1], to * nx + x).start()
        to_expert(m_send.at[to], m_col.at[z], zm_sem.at[0], zm_sem.at[1], to * nx + x).start()

    loop(1, nz, z_send)
    local(m_send.at[z], m_col.at[z], zm_sem.at[2]).start()
    loop(1, ne, scales_send)
    local(scl.at[ex], s_in.at[ex], sc_sem.at[2]).start()
    elements_send(0)
    encode(1)
    elements_send(1)

    many_z = pl.ds(0, nz - 1)
    local(xcol.at[many_z], xcol.at[many_z], z_sem.at[1]).wait()
    local(m_col.at[many_z], m_col.at[many_z], zm_sem.at[1]).wait()
    local(m_send.at[z], m_col.at[z], zm_sem.at[2]).wait()

    block4 = (lax.broadcasted_iota(jnp.int32, (2 * nx, gt), 1) // TOK * CAP).astype(F32)
    slot_of = lax.broadcasted_iota(jnp.int32, (gs, gt), 0).astype(F32)

    def targets(g):
        code = m_col[g, 0:2 * nx]
        return jnp.where(code > 0.5, block4 + code - 1.0, -1.0)

    def compact(g):
        tgt = targets(g)
        hot = jnp.concatenate([(slot_of == tgt[j:j + 1]).astype(F32) for j in range(2 * nx)], axis=0).astype(BF)
        taken = jnp.dot(hot, xcol[g], preferred_element_type=F32).astype(BF)
        for j in range(2 * nx):
            sbuf[j // 2, j % 2, pl.ds(pl.multiple_of(g * gs, gs), gs), :] = taken[j * gs:(j + 1) * gs]

    loop(0, nz, compact)

    for k in range(2):
        for j in range(1, nx):
            to = lax.rem(x + j, nx)
            to_expert(sbuf.at[to, k], slots.at[k, x], x_sem.at[0, k], x_sem.at[1, k], z * nx + to).start()
        local(sbuf.at[x, k], slots.at[k, x], x_sem.at[2, k]).start()

    for ph in range(2, 6):
        encode(ph)
        elements_send(ph)

    many_e = pl.ds(0, ne - 1)
    many_x = pl.ds(0, nx - 1)
    many_y = pl.ds(0, ny - 1)

    def elements_wait(ph):
        k, p = PHASES[ph]
        local(enc.at[ph, ex], got.at[ph, ex], e_own.at[ph]).wait()
        local(got.at[ph, many_e], got.at[ph, many_e], e_recv.at[ph]).wait()
        local(got.at[ph], out.at[k, p], e_out.at[ph]).start()

    def widen(ph, dst, base):
        sel = pick(ph)

        def step(i):
            at = pl.multiple_of(i * per * unit, per * unit)
            wide = jnp.dot(s_flat[pl.ds(at, per * unit), :], sel, preferred_element_type=F32)
            vals = [got[ph, i * per + u].astype(F32) * wide[u * unit:(u + 1) * unit] for u in range(per)]
            dst[pl.ds(base + at, per * unit), :] = jnp.concatenate(vals, axis=0).astype(BF)

        loop(0, ne // per, step)

    def gate_up(k, c, dst):
        lhs = slots[k, :, pl.ds(pl.multiple_of(c * half, half), half), :].reshape(nx * half, fs)
        cols = min(256, hidden)

        def step(n):
            at = pl.multiple_of(n * cols, cols)
            res = lax.dot_general(lhs, wgu[pl.ds(at, cols), :], (((1,), (1,)), ((), ())), preferred_element_type=F32)
            dst[k, :, :, pl.ds(at, cols)] = res.astype(BF).reshape(ny, half, cols)

        loop(0, 2 * hidden // cols, step)

    def first_sums(k):
        elements_wait(2 * k)
        widen(2 * k, wgu, 0)
        elements_wait(2 * k + 1)
        widen(2 * k + 1, wgu, hidden)
        local(slots.at[k, many_x], slots.at[k, many_x], x_sem.at[1, k]).wait()
        local(sbuf.at[x, k], slots.at[k, x], x_sem.at[2, k]).wait()
        gate_up(k, 1 - core, pa)
        to_fsdp(pa.at[k], ra.at[k], a_sem.at[0, k], a_sem.at[1, k], mate).start()
        gate_up(k, core, pb)
        local(pa.at[k], ra.at[k], a_sem.at[1, k]).wait()
        for j in range(ny):
            to = lax.rem(y + ny - 1 - j, ny)
            to = lax.rem(y + 1 + j, ny)
            rb[k, to] = (pb[k, to].astype(F32) + ra[k, to].astype(F32)).astype(BF)
            if j < ny - 1:
                to_fsdp(rb.at[k, to], rc.at[k, y], b_sem.at[0, k], b_sem.at[1, k], to * 2 + core).start()

    def activate(k):
        local(rc.at[k, many_y], rc.at[k, many_y], b_sem.at[1, k]).wait()
        total = rb[k, y].astype(F32)
        for j in range(1, ny):
            total = total + rc[k, lax.rem(y + j, ny)].astype(F32)
        gate, up = total[:, :hidden], total[:, hidden:]
        hid[k, core, y] = (gate / (1.0 + jnp.exp(-gate)) * up).astype(BF)
        for j in range(1, ny):
            to = lax.rem(y + j, ny)
            to_fsdp(hid.at[k, core, y], hid.at[k, core, y], h_sem.at[0, k], h_sem.at[1, k], to * 2 + core).start()

    def forward(k):
        local(hid.at[k, 0, many_y], hid.at[k, 0, many_y], h_sem.at[1, k]).wait()
        to_fsdp(hid.at[k, core], hid.at[k, core], i_sem.at[0, k], i_sem.at[1, k], mate).start()

    def down(k):
        local(hid.at[k, 0], hid.at[k, 0], i_sem.at[1, k]).wait()
        for j in range(nx):
            to = lax.rem(x + 1 + j, nx)
            lhs = jnp.concatenate([hid[k, 0, to], hid[k, 1, to]], axis=0)
            osend[k, to] = jnp.dot(lhs, wdn[...], preferred_element_type=F32).astype(BF)
            if j < nx - 1:
                to_expert(osend.at[k, to], orecv.at[k, x], o_sem.at[0, k], o_sem.at[1, k], z * nx + to).start()
            else:
                local(osend.at[k, to], orecv.at[k, to], o_sem.at[2, k]).start()

    local(scl.at[many_e], s_in.at[many_e], sc_sem.at[1]).wait()
    local(scl.at[ex], s_in.at[ex], sc_sem.at[2]).wait()

    def flatten(i):
        vals = [s_in[i * per + u].astype(F32) for u in range(per)]
        s_flat[pl.ds(pl.multiple_of(i * per * unit, per * unit), per * unit), :] = jnp.concatenate(vals, axis=0).astype(BF)

    loop(0, ne // per, flatten)

    first_sums(0)
    activate(0)
    forward(0)
    first_sums(1)
    elements_wait(4)
    widen(4, wdn, 0)
    down(0)
    activate(1)
    forward(1)
    elements_wait(5)
    widen(5, wdn, 0)
    down(1)

    for k in range(2):
        local(orecv.at[k, many_x], orecv.at[k, many_x], o_sem.at[1, k]).wait()
        local(osend.at[k, x], orecv.at[k, x], o_sem.at[2, k]).wait()

    def blend(j):
        g = lax.rem(z + j, nz)
        tgt = targets(g)
        share = m_col[g, 8:8 + 2 * nx]
        hot = jnp.concatenate([jnp.where(slot_of == tgt[i:i + 1], share[i:i + 1], 0.0) for i in range(2 * nx)], axis=0)
        hi = hot.astype(BF)
        lo = (hot - hi.astype(F32)).astype(BF)
        at = pl.ds(pl.multiple_of(g * gs, gs), gs)
        vals = jnp.concatenate([orecv[i % 2, i // 2, at, :] for i in range(2 * nx)], axis=0)
        both = (((0,), (0,)), ((), ()))
        part = lax.dot_general(hi, vals, both, preferred_element_type=F32)
        part = part + lax.dot_general(lo, vals, both, preferred_element_type=F32)
        pm[g] = part.astype(BF)

    def blend_send(j):
        blend(j)
        g = lax.rem(z + j, nz)
        to_expert(pm.at[g], pr.at[z], p_sem.at[0], p_sem.at[1], g * nx + x).start()

    loop(1, nz, blend_send)
    blend(0)
    local(pr.at[many_z], pr.at[many_z], p_sem.at[1]).wait()
    total = pm[z].astype(F32)
    for j in range(1, nz):
        total = total + pr[lax.rem(z + j, nz)].astype(F32)
    fin[...] = total.astype(BF)

    def fin_send(j):
        g = lax.rem(f + j, nf)
        to_fsdp(fin.at[pl.ds(pl.multiple_of(g * TOK, TOK), TOK)], mixed.at[:, pl.ds(pl.multiple_of(f * fs, fs), fs)],
                q_sem.at[0], q_sem.at[1], g).start()

    loop(1, nf, fin_send)
    mine = local(fin.at[here], mixed.at[:, pl.ds(pl.multiple_of(f * fs, fs), fs)], q_sem.at[2])
    mine.start()

    for ph, (k, p) in enumerate(PHASES):
        local(enc.at[ph, many_e], enc.at[ph, many_e], e_send.at[ph]).wait()
        local(got.at[ph], out.at[k, p], e_out.at[ph]).wait()
    local(scl.at[many_e], scl.at[many_e], sc_sem.at[0]).wait()
    local(xcol.at[z, many_f], xcol.at[z, many_f], t_sem.at[0]).wait()
    local(m_all.at[many_f], m_all.at[many_f], m_sem.at[0]).wait()
    local(xcol.at[many_z], xcol.at[many_z], z_sem.at[0]).wait()
    local(m_col.at[many_z], m_col.at[many_z], zm_sem.at[0]).wait()
    for k in range(2):
        local(slots.at[k, many_x], slots.at[k, many_x], x_sem.at[0, k]).wait()
        local(pa.at[k], pa.at[k], a_sem.at[0, k]).wait()
        local(rc.at[k, many_y], rc.at[k, many_y], b_sem.at[0, k]).wait()
        local(hid.at[k, 0, many_y], hid.at[k, 0, many_y], h_sem.at[0, k]).wait()
        local(hid.at[k, 0], hid.at[k, 0], i_sem.at[0, k]).wait()
        local(orecv.at[k, many_x], orecv.at[k, many_x], o_sem.at[0, k]).wait()
    local(pr.at[many_z], pr.at[many_z], p_sem.at[0]).wait()
    mine.wait()
    rest = mixed.at[:, pl.ds(0, (nf - 1) * fs)]
    local(rest, rest, q_sem.at[1]).wait()
    local(rest, rest, q_sem.at[0]).wait()


def run_layer(dims, rows, inv, scl, tok, meta):
    nz, nx, ny, fs, unit = dims
    ne, nf = nz * nx, 2 * ny
    gt, gs = nf * TOK, nf * CAP
    half, hidden = nz * gs // 2, ne * unit
    vm = pl.BlockSpec(memory_space=pltpu.VMEM)
    hbm = pl.BlockSpec(memory_space=pl.ANY)
    V = lambda *s: pltpu.VMEM(s, BF)
    dma = lambda *s: pltpu.SemaphoreType.DMA(s)
    return pl.pallas_call(
        functools.partial(layer, dims),
        out_shape=(jax.ShapeDtypeStruct((2, 3, ne, unit, fs), BF), jax.ShapeDtypeStruct((TOK, nf * fs), BF)),
        in_specs=[hbm, vm, vm, vm, vm],
        out_specs=(hbm, vm),
        scratch_shapes=[
            V(6, ne, unit, fs), V(6, ne, unit, fs), V(ne, unit, 128), V(hidden, 128),
            V(nz, gt, fs), pltpu.VMEM((gt, 128), F32), pltpu.VMEM((nz, 16, gt), F32), pltpu.VMEM((nz, 16, gt), F32),
            V(nx, 2, nz * gs, fs), V(2, nx, nz * gs, fs), V(2 * hidden, fs), V(hidden, fs),
            V(2, ny, half, 2 * hidden), V(2, ny, half, 2 * hidden), V(2, ny, half, 2 * hidden), V(2, ny, half, 2 * hidden), V(2, ny, half, 2 * hidden),
            V(2, 2, ny, half, hidden), V(2, nx, nz * gs, fs), V(2, nx, nz * gs, fs),
            V(nz, gt, fs), V(nz, gt, fs), V(gt, fs),
            dma(6), dma(6), dma(6), dma(6), dma(6), dma(3), dma(3), dma(3), dma(2), dma(3), dma(3, 2),
            dma(2, 2), dma(2, 2), dma(2, 2), dma(2, 2), dma(3, 2), dma(2), dma(3),
        ],
        compiler_params=pltpu.CompilerParams(collective_id=1, has_side_effects=True, vmem_limit_bytes=64000 * 1024),
        name="layer",
    )(rows, inv, scl, tok, meta)


def body(dims, tokens, learner_rows, exponents, expert_ids, route_probs):
    nz, nx, ny, fs, unit = dims
    ne = nz * nx
    nb = fs // BLOCK
    experts = 2 * ne
    exps = exponents.reshape(ne, 2, 3, unit, nb).transpose(0, 3, 1, 2, 4).reshape(ne, unit, 6 * nb).astype(F32)
    pad = ((0, 0), (0, 0), (0, 128 - 6 * nb))
    scl = jnp.pad(jnp.exp2(exps), pad).astype(BF)
    inv = jnp.pad(jnp.exp2(-exps), pad).astype(BF).reshape(ne * unit, 128)
    share = route_probs / jnp.sum(route_probs, axis=1, keepdims=True)
    hit = (expert_ids[:, :, None] == jnp.arange(experts, dtype=jnp.int32)).astype(F32)
    member = jnp.sum(hit, axis=1)
    weight = jnp.sum(hit * share[:, :, None], axis=1)
    order = jnp.arange(TOK)
    before = (order[None, :] < order[:, None]).astype(F32)
    code = member * (1.0 + jnp.dot(before, member))
    meta = jnp.zeros((TOK, 8, 16), F32)
    meta = meta.at[:, :nz, :2 * nx].set(code.reshape(TOK, nz, 2 * nx))
    meta = meta.at[:, :nz, 8:8 + 2 * nx].set(weight.reshape(TOK, nz, 2 * nx)).reshape(TOK, 128)
    el, mixed = run_layer(dims, learner_rows.reshape(ne, 2, 3, unit, fs), inv, scl, tokens, meta)
    return el.reshape(2, 3, ne * unit, fs), mixed


def make(mesh, dims):
    return jax.shard_map(
        functools.partial(body, dims),
        mesh=mesh,
        in_specs=(
            P(("fsdp", "expert"), None),
            P(None, None, "expert", "fsdp"),
            P(None, None, "expert", "fsdp"),
            P(("fsdp", "expert"), None),
            P(("fsdp", "expert"), None),
        ),
        out_specs=(P("expert", None, None, "fsdp"), P(("fsdp", "expert"), None)),
        check_vma=False,
    )


def solution(mesh):
    return make(mesh, (8, 4, 4, 512, 24))
```

```python
import functools
import jax
import jax.numpy as jnp
from jax import lax
from jax.experimental import pallas as pl
from jax.experimental.pallas import tpu as pltpu
from jax.sharding import PartitionSpec as P

BLOCK = 32
CAP = 4
NEAR = 20
VMEM_LIMIT = 64000 * 1024
TOK = 16
MESH = pl.DeviceIdType.MESH
BF, F32 = jnp.bfloat16, jnp.float32
PHASES = ((0, 0), (0, 1), (1, 0), (1, 1), (0, 2), (1, 2))
PARTS = ((0, 0, 2), (1, 0, 2), (2, 0, 2), (3, 0, 2), (4, 0, 1), (5, 0, 1), (4, 1, 1), (5, 1, 1))


def loop(low, high, step):
    def one(i, c):
        step(i)
        return c

    lax.fori_loop(low, high, one, 0)


def layer(dims, rows, exps, tok, packed, out, mixed,
          enc, got, inv_t, scl_t, s_out, s_in, meta, xcol, m_all, m_send, m_col, sbuf, slots, wgu, wdn,
          pa, pb, ra, rb, rc, hid, osend, orecv, pm, up_sum, dn_sum, fin,
          load_sem, e_send, e_recv, e_own, e_out, sc_sem, t_sem, m_sem, zu_sem, zd_sem, zm_sem, x_sem,
          x_own, a_sem, b_sem, h_sem, i_sem, o_sem, o_own, pu_sem, pd_sem, q_sem):
    nz, nx, ny, fs, unit = dims
    ne, nf = nz * nx, 2 * ny
    nb = fs // BLOCK
    gt, gs = nf * TOK, nf * CAP
    half = nz * gs // 2
    hidden = ne * unit
    wide_half = fs // 2
    chunk = half // 2
    experts, span = 2 * ne, unit * nb
    ups, downs = nz // 2, (nz - 1) // 2
    ex, f = lax.axis_index("expert"), lax.axis_index("fsdp")
    z, x = ex // nx, lax.rem(ex, nx)
    y, core = f // 2, lax.rem(f, 2)
    mate = y * 2 + (1 - core)
    barrier = pltpu.get_barrier_semaphore()

    def to_expert(src, dst, send, recv, e):
        return pltpu.make_async_remote_copy(src_ref=src, dst_ref=dst, send_sem=send, recv_sem=recv,
                                            device_id={"expert": e}, device_id_type=MESH)

    def to_fsdp(src, dst, send, recv, g):
        return pltpu.make_async_remote_copy(src_ref=src, dst_ref=dst, send_sem=send, recv_sem=recv,
                                            device_id={"fsdp": g}, device_id_type=MESH)

    def local(src, dst, sem):
        return pltpu.make_async_copy(src, dst, sem)

    def at_z(d):
        return lax.rem(z + d + nz, nz)

    for ph, (k, p) in enumerate(PHASES):
        local(rows.at[:, k, p], enc.at[ph], load_sem.at[ph]).start()

    def greet_expert(j):
        pl.semaphore_signal(barrier, inc=1, device_id={"expert": lax.rem(ex + j, ne)}, device_id_type=MESH)

    def greet_fsdp(j):
        pl.semaphore_signal(barrier, inc=1, device_id={"fsdp": lax.rem(f + j, nf)}, device_id_type=MESH)

    loop(1, nf, greet_fsdp)
    loop(1, ne, greet_expert)
    ids, probs = packed[0:8], packed[8:16]
    share = probs / jnp.sum(probs, axis=0, keepdims=True)
    expert_of = lax.broadcasted_iota(jnp.int32, (experts, 128), 0).astype(F32)
    member = jnp.zeros((experts, 128), F32)
    weight = jnp.zeros((experts, 128), F32)
    for i in range(8):
        hit = expert_of == ids[i:i + 1]
        member = member + hit.astype(F32)
        weight = weight + jnp.where(hit, share[i:i + 1], 0.0)
    before = lax.broadcasted_iota(jnp.int32, (128, 128), 0) < lax.broadcasted_iota(jnp.int32, (128, 128), 1)
    code = member * (1.0 + jnp.dot(member.astype(BF), before.astype(BF), preferred_element_type=F32))
    row_list = []
    for i in range(8):
        own = slice(i * 2 * nx, (i + 1) * 2 * nx)
        for table in (code, weight):
            if i < nz:
                row_list.append(table[own])
                if 2 * nx < 8:
                    row_list.append(jnp.zeros((8 - 2 * nx, 128), F32))
            else:
                row_list.append(jnp.zeros((8, 128), F32))
    meta[...] = jnp.transpose(jnp.concatenate(row_list, axis=0))[:TOK]

    for p in range(3):
        flat = exps[p].reshape(span, experts).astype(F32)
        if experts < 128:
            flat = jnp.concatenate([flat, jnp.zeros((span, 128 - experts), F32)], axis=1)
        turned = jnp.transpose(flat)[:experts]
        inv_t[p] = jnp.exp2(-turned).astype(BF).astype(F32)
        scl_t[p] = jnp.exp2(turned).astype(BF).astype(F32)

    def gather_scales(o):
        lines = [scl_t[p, pl.ds(o * 2 + k, 1), :] for k in range(2) for p in range(3)]
        s_out[o] = jnp.concatenate(lines + [jnp.zeros((2, span), F32)], axis=0).astype(BF)

    loop(0, ne, gather_scales)

    spread_row = lax.broadcasted_iota(jnp.int32, (unit, span), 0)
    spread_lane = lax.broadcasted_iota(jnp.int32, (unit, span), 1)
    diagonal = spread_lane // nb == spread_row

    def pick(at=0, width=None):
        width = width or fs
        lane = lax.broadcasted_iota(jnp.int32, (span, width), 0)
        feat = lax.broadcasted_iota(jnp.int32, (span, width), 1) + at
        return (lax.rem(lane, nb) == feat // BLOCK).astype(BF)

    per = min(8, ne)

    def encode(ph):
        local(rows.at[:, 0, 0], enc.at[ph], load_sem.at[ph]).wait()
        k, p = PHASES[ph]
        sel = pick()

        def step(i):
            lines = [jnp.where(diagonal, inv_t[p, pl.ds((i * per + u) * 2 + k, 1), :], 0.0) for u in range(per)]
            wide = jnp.dot(jnp.concatenate(lines, axis=0).astype(BF), sel, preferred_element_type=F32)
            for u in range(per):
                v = enc[ph, i * per + u].astype(F32) * wide[u * unit:(u + 1) * unit]
                v = jnp.minimum(jnp.maximum(v, -6.0), 6.0)
                a = jnp.abs(v)
                magic = jnp.where(a < 2.0, 6291456.0, jnp.where(a < 4.0, 12582912.0, 25165824.0))
                enc[ph, i * per + u] = ((v + magic) - magic).astype(BF)

        loop(0, ne // per, step)

    def zigzag(i):
        return lax.rem(ex + jnp.where(lax.rem(i, 2) == 1, (i + 1) // 2, ne - i // 2), ne)

    def part(n, ref, who):
        ph, lo, width = PARTS[n]
        return ref.at[ph, who] if width == 2 else ref.at[ph, who, :, pl.ds(lo * wide_half, wide_half)]

    def elements_some(n, low, high):
        def step(i):
            e = zigzag(i)
            to_expert(part(n, enc, e), part(n, got, ex), e_send.at[n], e_recv.at[n], e).start()

        loop(low, high, step)

    def elements_send(n):
        elements_some(n, 1, ne)
        local(part(n, enc, ex), part(n, got, ex), e_own.at[n]).start()

    def scales_send(i):
        e = zigzag(i)
        to_expert(s_out.at[e], s_in.at[ex], sc_sem.at[0], sc_sem.at[1], e).start()

    encode(0)
    encode(1)
    pl.semaphore_wait(barrier, ne + nf - 2)

    def tok_send(j):
        g = lax.rem(f + j, nf)
        here = pl.ds(pl.multiple_of(f * TOK, TOK), TOK)
        to_fsdp(tok.at[:, pl.ds(pl.multiple_of(g * fs, fs), fs)], xcol.at[z, here], t_sem.at[0], t_sem.at[1], g).start()
        to_fsdp(meta, m_all.at[here], m_sem.at[0], m_sem.at[1], g).start()

    here = pl.ds(pl.multiple_of(f * TOK, TOK), TOK)
    loop(1, nf, tok_send)
    local(tok.at[:, pl.ds(pl.multiple_of(f * fs, fs), fs)], xcol.at[z, here], t_sem.at[2]).start()
    local(meta, m_all.at[here], m_sem.at[2]).start()
    near = NEAR if ne > 16 else 2
    elements_some(0, 1, near)
    local(part(0, enc, ex), part(0, got, ex), e_own.at[0]).start()

    many_f = pl.ds(0, (nf - 1) * TOK)
    local(xcol.at[z, many_f], xcol.at[z, many_f], t_sem.at[1]).wait()
    local(xcol.at[z, here], xcol.at[z, here], t_sem.at[2]).wait()

    def cut(h, g):
        return xcol.at[g, :, pl.ds(h * wide_half, wide_half)]

    def push_up(h, step):
        g = at_z(1 - step)
        to_expert(cut(h, g), cut(h, g), zu_sem.at[0, h, step - 1], zu_sem.at[1, h, step - 1], at_z(1) * nx + x).start()

    def push_down(h, step):
        g = at_z(step - 1)
        to_expert(cut(h, g), cut(h, g), zd_sem.at[0, h, step - 1], zd_sem.at[1, h, step - 1], at_z(-1) * nx + x).start()

    for h in range(2):
        push_up(h, 1)
        if downs:
            push_down(h, 1)
    local(m_all.at[many_f], m_all.at[many_f], m_sem.at[1]).wait()
    local(meta, m_all.at[here], m_sem.at[2]).wait()
    turned = jnp.transpose(m_all[...])
    m_send[...] = turned.reshape(128 // 16, 16, gt)[:nz]

    def table_send(j):
        to = lax.rem(z + j, nz)
        to_expert(m_send.at[to], m_col.at[z], zm_sem.at[0], zm_sem.at[1], to * nx + x).start()

    loop(1, nz, table_send)
    local(m_send.at[z], m_col.at[z], zm_sem.at[2]).start()
    many_z = pl.ds(0, nz - 1)

    block4 = (lax.broadcasted_iota(jnp.int32, (2 * nx, gt), 1) // TOK * CAP).astype(F32)
    slot_of = lax.broadcasted_iota(jnp.int32, (gs, gt), 0).astype(F32)

    def targets(g):
        code = m_col[g, 0:2 * nx]
        return jnp.where(code > 0.5, block4 + code - 1.0, -1.0)

    def compact(g):
        tgt = targets(g)
        hot = jnp.concatenate([(slot_of == tgt[j:j + 1]).astype(F32) for j in range(2 * nx)], axis=0).astype(BF)
        taken = jnp.dot(hot, xcol[g], preferred_element_type=F32).astype(BF)
        at = pl.ds(pl.multiple_of(g * gs, gs), gs)
        for j in range(2 * nx):
            sbuf[j // 2, j % 2, at, :] = taken[j * gs:(j + 1) * gs]
        for j in range(1, nx):
            to = lax.rem(x + j, nx)
            to_expert(sbuf.at[to, 0, at], slots.at[0, x, at], x_sem.at[0, 0], x_sem.at[1, 0], z * nx + to).start()

    local(m_send.at[z], m_col.at[z], zm_sem.at[2]).wait()
    compact(z)
    for step in range(1, ups + 1):
        for h in range(2):
            local(cut(0, 0), cut(0, 0), zu_sem.at[1, h, step - 1]).wait()
            if step < ups:
                push_up(h, step + 1)
            if step <= downs:
                local(cut(0, 0), cut(0, 0), zd_sem.at[1, h, step - 1]).wait()
                if step < downs:
                    push_down(h, step + 1)
        if step == 1:
            local(m_col.at[many_z], m_col.at[many_z], zm_sem.at[1]).wait()
        if step == max(ups - 1, 1):
            loop(1, ne, scales_send)
            local(s_out.at[ex], s_in.at[ex], sc_sem.at[2]).start()
            elements_some(0, near, ne)
        compact(at_z(-step))
        if step <= downs:
            compact(at_z(step))

    local(sbuf.at[x, 0], slots.at[0, x], x_own.at[0]).start()
    elements_send(1)
    encode(2)
    elements_send(2)
    for j in range(1, nx):
        to = lax.rem(x + j, nx)
        to_expert(sbuf.at[to, 1], slots.at[1, x], x_sem.at[0, 1], x_sem.at[1, 1], z * nx + to).start()
    local(sbuf.at[x, 1], slots.at[1, x], x_own.at[1]).start()
    encode(3)
    elements_send(3)
    encode(4)
    elements_send(4)
    encode(5)
    for n in range(5, 8):
        elements_send(n)

    many_e = pl.ds(0, ne - 1)
    many_x = pl.ds(0, nx - 1)
    many_y = pl.ds(0, ny - 1)

    def elements_wait(n):
        ph, lo, width = PARTS[n]
        k, p = PHASES[ph]
        own, all_in = part(n, got, ex), part(n, got, many_e)
        local(own, own, e_own.at[n]).wait()
        local(all_in, all_in, e_recv.at[n]).wait()
        if lo + width == 2:
            local(got.at[ph], out.at[k, p], e_out.at[ph]).start()

    def widen(n, dst, base):
        ph, lo, width = PARTS[n]
        k, p = PHASES[ph]
        cols = width * wide_half
        sel = pick(lo * wide_half, cols)

        def step(i):
            at = pl.multiple_of(i * per * unit, per * unit)
            lines = [jnp.where(diagonal, s_in[i * per + u].astype(F32)[k * 3 + p:k * 3 + p + 1], 0.0) for u in range(per)]
            wide = jnp.dot(jnp.concatenate(lines, axis=0).astype(BF), sel, preferred_element_type=F32)
            vals = [got[ph, i * per + u, :, pl.ds(lo * wide_half, cols)].astype(F32) * wide[u * unit:(u + 1) * unit] for u in range(per)]
            dst[pl.ds(base + at, per * unit), :] = jnp.concatenate(vals, axis=0).astype(BF)

        loop(0, ne // per, step)

    def gate_up(k, c, dst, which):
        lhs = slots[k, :, pl.ds(pl.multiple_of(which * half + c * chunk, chunk), chunk), :].reshape(nx * chunk, fs)
        cols = min(256, hidden)

        def step(n):
            at = pl.multiple_of(n * cols, cols)
            res = lax.dot_general(lhs, wgu[pl.ds(at, cols), :], (((1,), (1,)), ((), ())), preferred_element_type=F32)
            dst[k, c, :, :, pl.ds(at, cols)] = res.astype(BF).reshape(ny, chunk, cols)

        loop(0, 2 * hidden // cols, step)

    def first_sums(k):
        elements_wait(2 * k)
        widen(2 * k, wgu, 0)
        elements_wait(2 * k + 1)
        widen(2 * k + 1, wgu, hidden)
        local(slots.at[k, many_x], slots.at[k, many_x], x_sem.at[1, k]).wait()
        local(sbuf.at[x, k], slots.at[k, x], x_own.at[k]).wait()
        for c in range(2):
            gate_up(k, c, pa, 1 - core)
            to_fsdp(pa.at[k, c], ra.at[k, c], a_sem.at[0, k, c], a_sem.at[1, k, c], mate).start()
            gate_up(k, c, pb, core)
        for c in range(2):
            local(pa.at[k, c], ra.at[k, c], a_sem.at[1, k, c]).wait()
            for j in range(ny):
                to = lax.rem(y + 1 + j, ny)
                rb[k, c, to] = (pb[k, c, to].astype(F32) + ra[k, c, to].astype(F32)).astype(BF)
                if j < ny - 1:
                    to_fsdp(rb.at[k, c, to], rc.at[k, c, y], b_sem.at[0, k, c], b_sem.at[1, k, c], to * 2 + core).start()

    def activate(k, c):
        local(rc.at[k, c, many_y], rc.at[k, c, many_y], b_sem.at[1, k, c]).wait()
        total = rb[k, c, y].astype(F32)
        for j in range(1, ny):
            total = total + rc[k, c, lax.rem(y + j, ny)].astype(F32)
        gate, up = total[:, :hidden], total[:, hidden:]
        hid[k, c, core, y] = (gate / (1.0 + jnp.exp(-gate)) * up).astype(BF)
        for j in range(1, ny):
            to = lax.rem(y + j, ny)
            to_fsdp(hid.at[k, c, core, y], hid.at[k, c, core, y], h_sem.at[0, k, c], h_sem.at[1, k, c], to * 2 + core).start()

    def forward(k, c):
        local(hid.at[k, c, 0, many_y], hid.at[k, c, 0, many_y], h_sem.at[1, k, c]).wait()
        to_fsdp(hid.at[k, c, core], hid.at[k, c, core], i_sem.at[0, k, c], i_sem.at[1, k, c], mate).start()

    def hidden_wait(k, c):
        local(hid.at[k, c, 0], hid.at[k, c, 0], i_sem.at[1, k, c]).wait()

    def down(k, h, c):
        for j in range(nx):
            to = lax.rem(x + 1 + j, nx)
            lhs = jnp.concatenate([hid[k, c, 0, to], hid[k, c, 1, to]], axis=0)
            osend[h, k, c, to] = jnp.dot(lhs, wdn[h], preferred_element_type=F32).astype(BF)
            if j < nx - 1:
                to_expert(osend.at[h, k, c, to], orecv.at[h, k, c, x], o_sem.at[0, h, k, c], o_sem.at[1, h, k, c], z * nx + to).start()
            else:
                local(osend.at[h, k, c, to], orecv.at[h, k, c, to], o_own.at[h, k, c]).start()

    def outputs_wait(h):
        for k in range(2):
            for c in range(2):
                local(orecv.at[h, k, c, many_x], orecv.at[h, k, c, many_x], o_sem.at[1, h, k, c]).wait()
                local(osend.at[h, k, c, x], orecv.at[h, k, c, x], o_own.at[h, k, c]).wait()

    def blend(h, g):
        tgt = targets(g)
        share = m_col[g, 8:8 + 2 * nx]
        hot = jnp.concatenate([jnp.where(slot_of == tgt[i:i + 1], share[i:i + 1], 0.0) for i in range(2 * nx)], axis=0)
        hi = hot.astype(BF)
        lo = (hot - hi.astype(F32)).astype(BF)
        which, inside = g // (nz // 2), lax.rem(g, nz // 2) * gs
        c, spot = inside // chunk, lax.rem(inside, chunk)
        at = pl.ds(pl.multiple_of(which * chunk + spot, gs), gs)
        vals = jnp.concatenate([orecv[h, i % 2, c, i // 2, at, :] for i in range(2 * nx)], axis=0)
        both = (((0,), (0,)), ((), ()))
        res = lax.dot_general(hi, vals, both, preferred_element_type=F32)
        return res + lax.dot_general(lo, vals, both, preferred_element_type=F32)

    def sum_up(h, step):
        g = at_z(ups + 1 - step)
        val = blend(h, g)
        if step > 1:
            local(up_sum.at[h, 0], up_sum.at[h, 0], pu_sem.at[1, h, step - 2]).wait()
            val = val + up_sum[h, step - 2].astype(F32)
        pm[h, 0, step - 1] = val.astype(BF)
        to_expert(pm.at[h, 0, step - 1], up_sum.at[h, step - 1], pu_sem.at[0, h, step - 1], pu_sem.at[1, h, step - 1], at_z(1) * nx + x).start()

    def sum_down(h, step):
        g = at_z(step - downs - 1)
        val = blend(h, g)
        if step > 1:
            local(dn_sum.at[h, 0], dn_sum.at[h, 0], pd_sem.at[1, h, step - 2]).wait()
            val = val + dn_sum[h, step - 2].astype(F32)
        pm[h, 1, step - 1] = val.astype(BF)
        to_expert(pm.at[h, 1, step - 1], dn_sum.at[h, step - 1], pd_sem.at[0, h, step - 1], pd_sem.at[1, h, step - 1], at_z(-1) * nx + x).start()

    def ring(h, step):
        sum_up(h, step)
        if step <= downs:
            sum_down(h, step)

    def finish(h):
        val = blend(h, z)
        local(up_sum.at[h, 0], up_sum.at[h, 0], pu_sem.at[1, h, ups - 1]).wait()
        val = val + up_sum[h, ups - 1].astype(F32)
        if downs:
            local(dn_sum.at[h, 0], dn_sum.at[h, 0], pd_sem.at[1, h, downs - 1]).wait()
            val = val + dn_sum[h, downs - 1].astype(F32)
        fin[h] = val.astype(BF)
        cols = pl.ds(pl.multiple_of(f * fs + h * wide_half, wide_half), wide_half)

        def fin_send(j):
            g = lax.rem(f + j, nf)
            to_fsdp(fin.at[h, pl.ds(pl.multiple_of(g * TOK, TOK), TOK)], mixed.at[:, cols], q_sem.at[0, h], q_sem.at[1, h], g).start()

        loop(1, nf, fin_send)
        local(fin.at[h, here], mixed.at[:, cols], q_sem.at[2, h]).start()

    local(s_in.at[many_e], s_in.at[many_e], sc_sem.at[1]).wait()
    local(s_out.at[ex], s_in.at[ex], sc_sem.at[2]).wait()

    first_sums(0)
    for c in range(2):
        activate(0, c)
    for c in range(2):
        forward(0, c)
    first_sums(1)
    elements_wait(4)
    widen(4, wdn.at[0], 0)
    for c in range(2):
        hidden_wait(0, c)
        down(0, 0, c)
    activate(1, 0)
    elements_wait(6)
    widen(6, wdn.at[1], 0)
    for c in range(2):
        down(0, 1, c)
    activate(1, 1)
    forward(1, 0)
    elements_wait(5)
    widen(5, wdn.at[0], 0)
    hidden_wait(1, 0)
    down(1, 0, 0)
    elements_wait(7)
    widen(7, wdn.at[1], 0)
    down(1, 1, 0)
    forward(1, 1)
    hidden_wait(1, 1)
    down(1, 0, 1)
    down(1, 1, 1)
    outputs_wait(0)
    ring(0, 1)
    outputs_wait(1)
    for step in range(1, ups + 1):
        ring(1, step)
        if step < ups:
            ring(0, step + 1)
    finish(0)
    finish(1)

    for n in range(8):
        out_n = part(n, enc, many_e)
        local(out_n, out_n, e_send.at[n]).wait()
    for ph, (k, p) in enumerate(PHASES):
        local(got.at[ph], out.at[k, p], e_out.at[ph]).wait()
    local(s_in.at[many_e], s_in.at[many_e], sc_sem.at[0]).wait()
    local(xcol.at[z, many_f], xcol.at[z, many_f], t_sem.at[0]).wait()
    local(m_all.at[many_f], m_all.at[many_f], m_sem.at[0]).wait()
    for h in range(2):
        for step in range(ups):
            local(cut(0, 0), cut(0, 0), zu_sem.at[0, h, step]).wait()
        for step in range(downs):
            local(cut(0, 0), cut(0, 0), zd_sem.at[0, h, step]).wait()
    local(m_col.at[many_z], m_col.at[many_z], zm_sem.at[0]).wait()
    for k in range(2):
        local(slots.at[k, many_x], slots.at[k, many_x], x_sem.at[0, k]).wait()
        for c in range(2):
            local(pa.at[k, c], pa.at[k, c], a_sem.at[0, k, c]).wait()
            local(rc.at[k, c, many_y], rc.at[k, c, many_y], b_sem.at[0, k, c]).wait()
            local(hid.at[k, c, 0, many_y], hid.at[k, c, 0, many_y], h_sem.at[0, k, c]).wait()
            local(hid.at[k, c, 0], hid.at[k, c, 0], i_sem.at[0, k, c]).wait()
    for h in range(2):
        for k in range(2):
            for c in range(2):
                local(orecv.at[h, k, c, many_x], orecv.at[h, k, c, many_x], o_sem.at[0, h, k, c]).wait()
        for step in range(ups):
            local(up_sum.at[h, 0], up_sum.at[h, 0], pu_sem.at[0, h, step]).wait()
        for step in range(downs):
            local(dn_sum.at[h, 0], dn_sum.at[h, 0], pd_sem.at[0, h, step]).wait()
        mine = fin.at[h, here]
        local(mine, mine, q_sem.at[2, h]).wait()
        rest = fin.at[h, many_f]
        local(rest, rest, q_sem.at[1, h]).wait()
        local(rest, rest, q_sem.at[0, h]).wait()


def run_layer(dims, rows, exps, tok, packed):
    nz, nx, ny, fs, unit = dims
    ne, nf = nz * nx, 2 * ny
    gt, gs = nf * TOK, nf * CAP
    half, hidden, ups = nz * gs // 2, ne * unit, nz // 2
    chunk, hw, span = half // 2, fs // 2, unit * (fs // BLOCK)
    vm = pl.BlockSpec(memory_space=pltpu.VMEM)
    hbm = pl.BlockSpec(memory_space=pl.ANY)
    V = lambda *s: pltpu.VMEM(s, BF)
    W = lambda *s: pltpu.VMEM(s, F32)
    dma = lambda *s: pltpu.SemaphoreType.DMA(s)
    sums = [V(2, 2, ny, chunk, 2 * hidden)] * 5
    return pl.pallas_call(
        functools.partial(layer, dims),
        out_shape=(jax.ShapeDtypeStruct((2, 3, ne, unit, fs), BF), jax.ShapeDtypeStruct((TOK, nf * fs), BF)),
        in_specs=[hbm, vm, vm, vm],
        out_specs=(hbm, vm),
        scratch_shapes=[
            V(6, ne, unit, fs), V(6, ne, unit, fs), W(3, 2 * ne, span), W(3, 2 * ne, span), V(ne, 8, span), V(ne, 8, span),
            W(TOK, 128), V(nz, gt, fs), W(gt, 128), W(nz, 16, gt), W(nz, 16, gt),
            V(nx, 2, nz * gs, fs), V(2, nx, nz * gs, fs), V(2 * hidden, fs), V(2, hidden, hw),
            *sums,
            V(2, 2, 2, ny, chunk, hidden), V(2, 2, 2, nx, 2 * chunk, hw), V(2, 2, 2, nx, 2 * chunk, hw),
            V(2, 2, ups, gt, hw), V(2, ups, gt, hw), V(2, ups, gt, hw), V(2, gt, hw),
            dma(6), dma(8), dma(8), dma(8), dma(6), dma(3), dma(3), dma(3), dma(2, 2, ups), dma(2, 2, ups), dma(3), dma(2, 2), dma(2),
            dma(2, 2, 2), dma(2, 2, 2), dma(2, 2, 2), dma(2, 2, 2), dma(2, 2, 2, 2), dma(2, 2, 2), dma(2, 2, ups), dma(2, 2, ups), dma(3, 2),
        ],
        compiler_params=pltpu.CompilerParams(collective_id=1, has_side_effects=True, vmem_limit_bytes=VMEM_LIMIT),
        name="layer",
    )(rows, exps, tok, packed)


def body(dims, tokens, learner_rows, exponents, expert_ids, route_probs):
    nz, nx, ny, fs, unit = dims
    ne = nz * nx
    top = expert_ids.shape[1]
    ids = jnp.pad(expert_ids.T.astype(F32), ((0, 8 - top), (0, 128 - TOK)), constant_values=-1.0)
    probs = jnp.pad(jnp.pad(route_probs.T, ((0, 8 - top), (0, 0))), ((0, 0), (0, 128 - TOK)), constant_values=1.0)
    packed = jnp.concatenate([ids, probs], axis=0)
    el, mixed = run_layer(dims, learner_rows.reshape(ne, 2, 3, unit, fs), exponents.transpose(1, 2, 3, 0), tokens, packed)
    return el.reshape(2, 3, ne * unit, fs), mixed


def make(mesh, dims):
    return jax.shard_map(
        functools.partial(body, dims),
        mesh=mesh,
        in_specs=(
            P(("fsdp", "expert"), None),
            P(None, None, "expert", "fsdp"),
            P(None, None, "expert", "fsdp"),
            P(("fsdp", "expert"), None),
            P(("fsdp", "expert"), None),
        ),
        out_specs=(P("expert", None, None, "fsdp"), P(("fsdp", "expert"), None)),
        check_vma=False,
    )


def solution(mesh):
    return make(mesh, (8, 4, 4, 512, 24))
```

```python
import functools
import jax
import jax.numpy as jnp
from jax import lax
from jax.experimental import pallas as pl
from jax.experimental.pallas import tpu as pltpu
from jax.sharding import PartitionSpec as P

BLOCK = 32
CAP = 4
NEAR = 20
SLICES = ((0, 20, 26), (0, 26, 32), (1, 1, 16), (1, 16, 24), (1, 24, 32))
VMEM_LIMIT = 47 * 1024 * 1024
TOK = 16
MESH = pl.DeviceIdType.MESH
BF, F32 = jnp.bfloat16, jnp.float32
PHASES = ((0, 0), (0, 1), (1, 0), (1, 1), (0, 2), (1, 2))
PIECES = 2
PARTS = tuple((ph, 0, PIECES) for ph in range(4)) + tuple((ph, h, 1) for ph in (4, 5) for h in range(PIECES))


def loop(low, high, step):
    def one(i, c):
        step(i)
        return c

    lax.fori_loop(low, high, one, 0)


def layer(dims, rows, exps_in, tok_in, ids_in, probs_in, out, mixed,
          enc, exps, tok, ids_raw, probs_raw, inv_t, scl_t, s_out, s_in, meta, mix, xcol, m_all, m_send, m_col, sbuf, slots, wgu, wdn,
          pa, pb, ra, rb, rc, rl, hid, osend, orecv, pm, up_sum, dn_sum, fin,
          load_sem, in_sem, e_send, e_recv, e_own, sc_sem, t_sem, m_sem, zu_sem, zd_sem, zm_sem, x_sem,
          x_own, a_sem, b_sem, h_sem, i_sem, o_sem, o_own, pu_sem, pd_sem, q_sem):
    nz, nx, ny, fs, unit = dims
    ne, nf = nz * nx, 2 * ny
    nb = fs // BLOCK
    gt, gs = nf * TOK, nf * CAP
    half = nz * gs // 2
    hidden = ne * unit
    wide_half = fs // PIECES
    ring_half = fs // 2
    chunk = half // 2
    experts, span = 2 * ne, unit * nb
    ups, downs = nz // 2, (nz - 1) // 2
    ex, f = lax.axis_index("expert"), lax.axis_index("fsdp")
    z, x = ex // nx, lax.rem(ex, nx)
    y, core = f // 2, lax.rem(f, 2)
    mate = y * 2 + (1 - core)
    barrier = pltpu.get_barrier_semaphore()

    def to_expert(src, dst, send, recv, e):
        return pltpu.make_async_remote_copy(src_ref=src, dst_ref=dst, send_sem=send, recv_sem=recv,
                                            device_id={"expert": e}, device_id_type=MESH)

    def to_fsdp(src, dst, send, recv, g):
        return pltpu.make_async_remote_copy(src_ref=src, dst_ref=dst, send_sem=send, recv_sem=recv,
                                            device_id={"fsdp": g}, device_id_type=MESH)

    def local(src, dst, sem):
        return pltpu.make_async_copy(src, dst, sem)

    def at_z(d):
        return lax.rem(z + d + nz, nz)

    small = [local(src, dst, in_sem.at[i]) for i, (src, dst) in enumerate(
        ((ids_in, ids_raw), (probs_in, probs_raw), (exps_in, exps), (tok_in, tok)))]

    def greet_expert(j):
        pl.semaphore_signal(barrier, inc=1, device_id={"expert": lax.rem(ex + j, ne)}, device_id_type=MESH)

    def greet_fsdp(j):
        pl.semaphore_signal(barrier, inc=1, device_id={"fsdp": lax.rem(f + j, nf)}, device_id_type=MESH)

    loop(1, nf, greet_fsdp)
    loop(1, ne, greet_expert)
    for copy in small:
        copy.start()
    for ph, (k, p) in enumerate(PHASES):
        local(rows.at[:, k, p], enc.at[ph], load_sem.at[ph]).start()

    small[0].wait()
    small[1].wait()
    top = ids_raw.shape[0]
    widen_lanes = (lax.broadcasted_iota(jnp.int32, (TOK, 128), 0) == lax.broadcasted_iota(jnp.int32, (TOK, 128), 1)).astype(F32)
    ids = jnp.dot(ids_raw[...].astype(F32), widen_lanes, precision=lax.Precision.HIGHEST, preferred_element_type=F32)
    probs = probs_raw[...] / jnp.sum(probs_raw[...], axis=0, keepdims=True)
    share = jnp.dot(probs, widen_lanes, precision=lax.Precision.HIGHEST, preferred_element_type=F32)
    expert_of = lax.broadcasted_iota(jnp.int32, (experts, 128), 0).astype(F32)
    member = jnp.zeros((experts, 128), F32)
    weight = jnp.zeros((experts, 128), F32)
    for i in range(top):
        hit = expert_of == ids[i:i + 1]
        member = member + hit.astype(F32)
        weight = weight + jnp.where(hit, share[i:i + 1], 0.0)
    before = lax.broadcasted_iota(jnp.int32, (128, 128), 0) < lax.broadcasted_iota(jnp.int32, (128, 128), 1)
    code = member * (1.0 + jnp.dot(member.astype(BF), before.astype(BF), preferred_element_type=F32))
    row_list = []
    for i in range(8):
        own = slice(i * 2 * nx, (i + 1) * 2 * nx)
        for table in (code, weight):
            if i < nz:
                row_list.append(table[own])
                if 2 * nx < 8:
                    row_list.append(jnp.zeros((8 - 2 * nx, 128), F32))
            else:
                row_list.append(jnp.zeros((8, 128), F32))
    meta[...] = jnp.transpose(jnp.concatenate(row_list, axis=0))[:TOK]

    small[2].wait()
    for p in range(3):
        flat = exps[p].reshape(span, experts).astype(F32)
        if experts < 128:
            flat = jnp.concatenate([flat, jnp.zeros((span, 128 - experts), F32)], axis=1)
        turned = jnp.transpose(flat)[:experts]
        inv_t[p] = jnp.exp2(-turned).astype(BF).astype(F32)
        scl_t[p] = jnp.exp2(turned).astype(BF).astype(F32)

    def gather_scales(o):
        lines = [scl_t[p, pl.ds(o * 2 + k, 1), :] for k in range(2) for p in range(3)]
        s_out[o] = jnp.concatenate(lines + [jnp.zeros((2, span), F32)], axis=0).astype(BF)

    loop(0, ne, gather_scales)

    spread_row = lax.broadcasted_iota(jnp.int32, (unit, span), 0)
    spread_lane = lax.broadcasted_iota(jnp.int32, (unit, span), 1)
    diagonal = spread_lane // nb == spread_row

    def pick(at=0, width=None):
        width = width or fs
        lane = lax.broadcasted_iota(jnp.int32, (span, width), 0)
        feat = lax.broadcasted_iota(jnp.int32, (span, width), 1) + at
        return (lax.rem(lane, nb) == feat // BLOCK).astype(BF)

    per = min(8, ne)

    def encode(ph):
        local(rows.at[:, 0, 0], enc.at[ph], load_sem.at[ph]).wait()
        k, p = PHASES[ph]
        sel = pick()

        def step(i):
            lines = [jnp.where(diagonal, inv_t[p, pl.ds((i * per + u) * 2 + k, 1), :], 0.0) for u in range(per)]
            wide = jnp.dot(jnp.concatenate(lines, axis=0).astype(BF), sel, preferred_element_type=F32)
            for u in range(per):
                v = enc[ph, i * per + u].astype(F32) * wide[u * unit:(u + 1) * unit]
                v = jnp.minimum(jnp.maximum(v, -6.0), 6.0)
                a = jnp.abs(v)
                magic = jnp.where(a < 2.0, 6291456.0, jnp.where(a < 4.0, 12582912.0, 25165824.0))
                enc[ph, i * per + u] = ((v + magic) - magic).astype(BF)

        loop(0, ne // per, step)

    def zigzag(i):
        return lax.rem(ex + jnp.where(lax.rem(i, 2) == 1, (i + 1) // 2, ne - i // 2), ne)

    def part(n, ref, who):
        ph, lo, width = PARTS[n]
        mine = ref.at[ph] if ref is enc else ref.at[PHASES[ph][0], PHASES[ph][1]]
        return mine.at[who] if width == PIECES else mine.at[who, :, pl.ds(lo * wide_half, wide_half)]

    def elements_some(n, low, high):
        def step(i):
            e = zigzag(i)
            to_expert(part(n, enc, e), part(n, out, ex), e_send.at[n], e_recv.at[n], e).start()

        loop(low, high, step)

    def elements_send(n):
        elements_some(n, 1, ne)
        local(part(n, enc, ex), part(n, out, ex), e_own.at[n]).start()

    def scales_send(i):
        e = zigzag(i)
        to_expert(s_out.at[e], s_in.at[ex], sc_sem.at[0], sc_sem.at[1], e).start()

    encode(0)
    encode(1)
    small[3].wait()
    pl.semaphore_wait(barrier, ne + nf - 2)

    def tok_send(j):
        g = lax.rem(f + j, nf)
        here = pl.ds(pl.multiple_of(f * TOK, TOK), TOK)
        to_fsdp(tok.at[:, pl.ds(pl.multiple_of(g * fs, fs), fs)], xcol.at[z, here], t_sem.at[0], t_sem.at[1], g).start()
        to_fsdp(meta, m_all.at[here], m_sem.at[0], m_sem.at[1], g).start()

    here = pl.ds(pl.multiple_of(f * TOK, TOK), TOK)
    loop(1, nf, tok_send)
    local(tok.at[:, pl.ds(pl.multiple_of(f * fs, fs), fs)], xcol.at[z, here], t_sem.at[2]).start()
    local(meta, m_all.at[here], m_sem.at[2]).start()
    near = NEAR if ups == 4 else 2
    elements_some(0, 1, near)
    local(part(0, enc, ex), part(0, out, ex), e_own.at[0]).start()

    many_f = pl.ds(0, (nf - 1) * TOK)
    local(xcol.at[z, many_f], xcol.at[z, many_f], t_sem.at[1]).wait()
    local(xcol.at[z, here], xcol.at[z, here], t_sem.at[2]).wait()

    def cut(h, g):
        return xcol.at[g, :, pl.ds(h * ring_half, ring_half)]

    def push_up(h, step):
        g = at_z(1 - step)
        to_expert(cut(h, g), cut(h, g), zu_sem.at[0, h, step - 1], zu_sem.at[1, h, step - 1], at_z(1) * nx + x).start()

    def push_down(h, step):
        g = at_z(step - 1)
        to_expert(cut(h, g), cut(h, g), zd_sem.at[0, h, step - 1], zd_sem.at[1, h, step - 1], at_z(-1) * nx + x).start()

    for h in range(2):
        push_up(h, 1)
        if downs:
            push_down(h, 1)
    local(m_all.at[many_f], m_all.at[many_f], m_sem.at[1]).wait()
    local(meta, m_all.at[here], m_sem.at[2]).wait()
    turned = jnp.transpose(m_all[...])
    m_send[...] = turned.reshape(128 // 16, 16, gt)[:nz]

    def table_send(j):
        to = lax.rem(z + j, nz)
        to_expert(m_send.at[to], m_col.at[z], zm_sem.at[0], zm_sem.at[1], to * nx + x).start()

    loop(1, nz, table_send)
    local(m_send.at[z], m_col.at[z], zm_sem.at[2]).start()
    many_z = pl.ds(0, nz - 1)

    block4 = (lax.broadcasted_iota(jnp.int32, (2 * nx, gt), 1) // TOK * CAP).astype(F32)
    slot_of = lax.broadcasted_iota(jnp.int32, (gs, gt), 0).astype(F32)

    def targets(g):
        code = m_col[g, 0:2 * nx]
        return jnp.where(code > 0.5, block4 + code - 1.0, -1.0)

    def compact(g):
        tgt = targets(g)
        hot = jnp.concatenate([(slot_of == tgt[j:j + 1]).astype(F32) for j in range(2 * nx)], axis=0).astype(BF)
        taken = jnp.dot(hot, xcol[g], preferred_element_type=F32).astype(BF)
        at = pl.ds(pl.multiple_of(g * gs, gs), gs)
        for j in range(2 * nx):
            sbuf[j // 2, j % 2, at, :] = taken[j * gs:(j + 1) * gs]
        for j in range(1, nx):
            to = lax.rem(x + j, nx)
            to_expert(sbuf.at[to, 0, at], slots.at[0, x, at], x_sem.at[0, 0], x_sem.at[1, 0], z * nx + to).start()

    local(m_send.at[z], m_col.at[z], zm_sem.at[2]).wait()
    compact(z)
    for step in range(1, ups + 1):
        for h in range(2):
            local(cut(0, 0), cut(0, 0), zu_sem.at[1, h, step - 1]).wait()
            if step < ups:
                push_up(h, step + 1)
            if step <= downs:
                local(cut(0, 0), cut(0, 0), zd_sem.at[1, h, step - 1]).wait()
                if step < downs:
                    push_down(h, step + 1)
        if step == 1:
            local(m_col.at[many_z], m_col.at[many_z], zm_sem.at[1]).wait()
        if step == max(ups - 1, 1):
            loop(1, ne, scales_send)
            local(s_out.at[ex], s_in.at[ex], sc_sem.at[2]).start()
        if ups == 4:
            elements_some(*SLICES[step - 1])
        compact(at_z(-step))
        if step <= downs:
            compact(at_z(step))

    local(sbuf.at[x, 0], slots.at[0, x], x_own.at[0]).start()
    if ups == 4:
        elements_some(*SLICES[4])
        local(part(1, enc, ex), part(1, out, ex), e_own.at[1]).start()
    else:
        elements_some(0, near, ne)
        elements_send(1)
    encode(2)
    elements_send(2)
    for j in range(1, nx):
        to = lax.rem(x + j, nx)
        to_expert(sbuf.at[to, 1], slots.at[1, x], x_sem.at[0, 1], x_sem.at[1, 1], z * nx + to).start()
    local(sbuf.at[x, 1], slots.at[1, x], x_own.at[1]).start()
    for ph in range(3, 6):
        encode(ph)

    many_e = pl.ds(0, ne - 1)
    many_x = pl.ds(0, nx - 1)
    many_y = pl.ds(0, ny - 1)

    def elements_wait(n):
        own, all_in = part(n, out, ex), part(n, out, many_e)
        local(own, own, e_own.at[n]).wait()
        local(all_in, all_in, e_recv.at[n]).wait()

    def widen(n, dst, base):
        ph, lo, width = PARTS[n]
        k, p = PHASES[ph]
        cols = width * wide_half
        sel = pick(lo * wide_half, cols)

        def step(i):
            at = pl.multiple_of(i * per * unit, per * unit)
            lines = [jnp.where(diagonal, s_in[i * per + u].astype(F32)[k * 3 + p:k * 3 + p + 1], 0.0) for u in range(per)]
            wide = jnp.dot(jnp.concatenate(lines, axis=0).astype(BF), sel, preferred_element_type=F32)
            vals = [out[k, p, i * per + u, :, pl.ds(lo * wide_half, cols)].astype(F32) * wide[u * unit:(u + 1) * unit] for u in range(per)]
            dst[pl.ds(base + at, per * unit), :] = jnp.concatenate(vals, axis=0).astype(BF)

        loop(0, ne // per, step)

    cols = min(256, hidden)

    def gate_up(k, c, dst, which, base):
        lhs = slots[k, :, pl.ds(pl.multiple_of(which * half + c * chunk, chunk), chunk), :].reshape(nx * chunk, fs)

        def step(n):
            at = pl.multiple_of(base + n * cols, cols)
            res = lax.dot_general(lhs, wgu[pl.ds(at, cols), :], (((1,), (1,)), ((), ())), preferred_element_type=F32)
            dst[k, c, :, :, pl.ds(at, cols)] = res.astype(BF).reshape(ny, chunk, cols)

        loop(0, hidden // cols, step)

    def gates(k):
        elements_wait(2 * k)
        widen(2 * k, wgu, 0)
        local(slots.at[k, many_x], slots.at[k, many_x], x_sem.at[1, k]).wait()
        local(sbuf.at[x, k], slots.at[k, x], x_own.at[k]).wait()
        for c in range(2):
            gate_up(k, c, pa, 1 - core, 0)
            gate_up(k, c, pb, core, 0)

    def first_sums(k):
        elements_wait(2 * k + 1)
        widen(2 * k + 1, wgu, hidden)
        for c in range(2):
            gate_up(k, c, pa, 1 - core, hidden)
            to_fsdp(pa.at[k, c], ra.at[k, c], a_sem.at[0, k, c], a_sem.at[1, k, c], mate).start()
            gate_up(k, c, pb, core, hidden)
        for c in range(2):
            local(pa.at[k, c], ra.at[k, c], a_sem.at[1, k, c]).wait()
            for j in ((2, 1, 3, 0) if ny == 4 else (1, 0)):
                to = lax.rem(y + j, ny)
                rb[k, c, to] = (pb[k, c, to].astype(F32) + ra[k, c, to].astype(F32)).astype(BF)
                if ny == 4 and j == 2:
                    for d in range(2):
                        side = rb.at[k, c, to, :, pl.ds(d * hidden, hidden)]
                        to_fsdp(side, rl.at[k, c, d], b_sem.at[0, k, c, d], b_sem.at[1, k, c, d], beside(d)).start()
            if ny != 4:
                to_fsdp(rb.at[k, c, 1 - y], rc.at[k, c, 0], b_sem.at[0, k, c, 2], b_sem.at[1, k, c, 2], (1 - y) * 2 + core).start()

    def beside(d):
        return lax.rem(y + (1 if d == 0 else ny - 1), ny) * 2 + core

    def relay(k, c):
        if ny != 4:
            return
        for d in range(2):
            local(rl.at[k, c, d], rl.at[k, c, d], b_sem.at[1, k, c, d]).wait()
            to = lax.rem(y + (1 if d == 0 else ny - 1), ny)
            side = pl.ds(d * hidden, hidden)
            rb[k, c, to, :, side] = (rb[k, c, to, :, side].astype(F32) + rl[k, c, d].astype(F32)).astype(BF)
            to_fsdp(rb.at[k, c, to], rc.at[k, c, d], b_sem.at[0, k, c, 2 + d], b_sem.at[1, k, c, 2 + d], beside(d)).start()

    def activate(k, c):
        total = rb[k, c, y].astype(F32)
        for d in range(2 if ny == 4 else 1):
            local(rc.at[k, c, d], rc.at[k, c, d], b_sem.at[1, k, c, 2 + d]).wait()
            total = total + rc[k, c, d].astype(F32)
        gate, up = total[:, :hidden], total[:, hidden:]
        hid[k, c, core, y] = (gate / (1.0 + jnp.exp(-gate)) * up).astype(BF)
        for j in range(1, ny):
            to = lax.rem(y + j, ny)
            to_fsdp(hid.at[k, c, core, y], hid.at[k, c, core, y], h_sem.at[0, k, c], h_sem.at[1, k, c], to * 2 + core).start()

    def forward(k, c):
        local(hid.at[k, c, 0, many_y], hid.at[k, c, 0, many_y], h_sem.at[1, k, c]).wait()
        to_fsdp(hid.at[k, c, core], hid.at[k, c, core], i_sem.at[0, k, c], i_sem.at[1, k, c], mate).start()

    def hidden_wait(k, c):
        local(hid.at[k, c, 0], hid.at[k, c, 0], i_sem.at[1, k, c]).wait()

    def down(k, h, c):
        for j in range(nx):
            to = lax.rem(x + 1 + j, nx)
            lhs = jnp.concatenate([hid[k, c, 0, to], hid[k, c, 1, to]], axis=0)
            osend[h, k, c, to] = jnp.dot(lhs, wdn[h], preferred_element_type=F32).astype(BF)
            if j < nx - 1:
                to_expert(osend.at[h, k, c, to], orecv.at[h, k, c, x], o_sem.at[0, h, k, c], o_sem.at[1, h, k, c], z * nx + to).start()
            else:
                local(osend.at[h, k, c, to], orecv.at[h, k, c, to], o_own.at[h, k, c]).start()

    def outputs_wait(h):
        for k in range(2):
            for c in range(2):
                local(orecv.at[h, k, c, many_x], orecv.at[h, k, c, many_x], o_sem.at[1, h, k, c]).wait()
                local(osend.at[h, k, c, x], orecv.at[h, k, c, x], o_own.at[h, k, c]).wait()

    def blend(h, g):
        tgt = targets(g)
        share = m_col[g, 8:8 + 2 * nx]
        hot = jnp.concatenate([jnp.where(slot_of == tgt[i:i + 1], share[i:i + 1], 0.0) for i in range(2 * nx)], axis=0)
        hi = hot.astype(BF)
        lo = (hot - hi.astype(F32)).astype(BF)
        which, inside = g // (nz // 2), lax.rem(g, nz // 2) * gs
        c, spot = inside // chunk, lax.rem(inside, chunk)
        at = pl.ds(pl.multiple_of(which * chunk + spot, gs), gs)
        vals = jnp.concatenate([orecv[h, i % 2, c, i // 2, at, :] for i in range(2 * nx)], axis=0)
        both = (((0,), (0,)), ((), ()))
        res = lax.dot_general(hi, vals, both, preferred_element_type=F32)
        return res + lax.dot_general(lo, vals, both, preferred_element_type=F32)

    def blend_rest(h):
        for d in range(nz):
            if d not in (ups, downs + 2):
                mix[h, d] = blend(h, at_z(d))

    def sum_up(h, step):
        val = mix[h, ups + 1 - step]
        if step > 1:
            local(up_sum.at[h, 0], up_sum.at[h, 0], pu_sem.at[1, h, step - 2]).wait()
            val = val + up_sum[h, step - 2].astype(F32)
        pm[h, 0, step - 1] = val.astype(BF)
        to_expert(pm.at[h, 0, step - 1], up_sum.at[h, step - 1], pu_sem.at[0, h, step - 1], pu_sem.at[1, h, step - 1], at_z(1) * nx + x).start()

    def sum_down(h, step):
        val = mix[h, nz + step - downs - 1]
        if step > 1:
            local(dn_sum.at[h, 0], dn_sum.at[h, 0], pd_sem.at[1, h, step - 2]).wait()
            val = val + dn_sum[h, step - 2].astype(F32)
        pm[h, 1, step - 1] = val.astype(BF)
        to_expert(pm.at[h, 1, step - 1], dn_sum.at[h, step - 1], pd_sem.at[0, h, step - 1], pd_sem.at[1, h, step - 1], at_z(-1) * nx + x).start()

    def ring(h, step):
        sum_up(h, step)
        if step <= downs:
            sum_down(h, step)

    def finish(h):
        val = mix[h, 0]
        local(up_sum.at[h, 0], up_sum.at[h, 0], pu_sem.at[1, h, ups - 1]).wait()
        val = val + up_sum[h, ups - 1].astype(F32)
        if downs:
            local(dn_sum.at[h, 0], dn_sum.at[h, 0], pd_sem.at[1, h, downs - 1]).wait()
            val = val + dn_sum[h, downs - 1].astype(F32)
        fin[h] = val.astype(BF)
        cols = pl.ds(pl.multiple_of(f * fs + h * wide_half, wide_half), wide_half)

        def fin_send(j):
            g = lax.rem(f + j, nf)
            to_fsdp(fin.at[h, pl.ds(pl.multiple_of(g * TOK, TOK), TOK)], mixed.at[:, cols], q_sem.at[0, h], q_sem.at[1, h], g).start()

        loop(1, nf, fin_send)
        local(fin.at[h, here], mixed.at[:, cols], q_sem.at[2, h]).start()

    local(s_in.at[many_e], s_in.at[many_e], sc_sem.at[1]).wait()
    local(s_out.at[ex], s_in.at[ex], sc_sem.at[2]).wait()

    gates(0)
    elements_send(3)
    first_sums(0)
    relay(0, 0)
    relay(0, 1)
    gates(1)
    for n in range(4, 4 + PIECES):
        elements_send(n)
    activate(0, 0)
    activate(0, 1)
    first_sums(1)
    for n in range(4 + PIECES, len(PARTS)):
        elements_send(n)
    for c in range(2):
        forward(0, c)
    relay(1, 0)
    relay(1, 1)
    for h in range(PIECES):
        elements_wait(4 + h)
        widen(4 + h, wdn.at[h], 0)
        for c in range(2):
            if h == 0:
                hidden_wait(0, c)
            down(0, h, c)
        if h == 0:
            activate(1, 0)
    activate(1, 1)
    forward(1, 0)
    for h in range(PIECES):
        elements_wait(4 + PIECES + h)
        widen(4 + PIECES + h, wdn.at[h], 0)
        if h == 0:
            hidden_wait(1, 0)
        down(1, h, 0)
        if h == 0:
            forward(1, 1)
            hidden_wait(1, 1)
        down(1, h, 1)
    for t in range(PIECES + ups):
        for h in range(PIECES):
            step = t - h + 1
            if step == 1:
                outputs_wait(h)
                for d in (ups, downs + 2) if downs else (ups,):
                    mix[h, d] = blend(h, at_z(d))
            if 1 <= step <= ups:
                ring(h, step)
            if step == 1:
                blend_rest(h)
            if step == ups + 1:
                finish(h)

    for n in range(len(PARTS)):
        out_n = part(n, enc, many_e)
        local(out_n, out_n, e_send.at[n]).wait()
    local(s_in.at[many_e], s_in.at[many_e], sc_sem.at[0]).wait()
    local(xcol.at[z, many_f], xcol.at[z, many_f], t_sem.at[0]).wait()
    local(m_all.at[many_f], m_all.at[many_f], m_sem.at[0]).wait()
    for h in range(2):
        for step in range(ups):
            local(cut(0, 0), cut(0, 0), zu_sem.at[0, h, step]).wait()
        for step in range(downs):
            local(cut(0, 0), cut(0, 0), zd_sem.at[0, h, step]).wait()
    local(m_col.at[many_z], m_col.at[many_z], zm_sem.at[0]).wait()
    for k in range(2):
        local(slots.at[k, many_x], slots.at[k, many_x], x_sem.at[0, k]).wait()
        for c in range(2):
            local(pa.at[k, c], pa.at[k, c], a_sem.at[0, k, c]).wait()
            for d in range(2 if ny == 4 else 1):
                local(rc.at[k, c, d], rc.at[k, c, d], b_sem.at[0, k, c, 2 + d]).wait()
                if ny == 4:
                    local(rl.at[k, c, d], rl.at[k, c, d], b_sem.at[0, k, c, d]).wait()
            local(hid.at[k, c, 0, many_y], hid.at[k, c, 0, many_y], h_sem.at[0, k, c]).wait()
            local(hid.at[k, c, 0], hid.at[k, c, 0], i_sem.at[0, k, c]).wait()
    for h in range(PIECES):
        for k in range(2):
            for c in range(2):
                local(orecv.at[h, k, c, many_x], orecv.at[h, k, c, many_x], o_sem.at[0, h, k, c]).wait()
        for step in range(ups):
            local(up_sum.at[h, 0], up_sum.at[h, 0], pu_sem.at[0, h, step]).wait()
        for step in range(downs):
            local(dn_sum.at[h, 0], dn_sum.at[h, 0], pd_sem.at[0, h, step]).wait()
        mine = fin.at[h, here]
        local(mine, mine, q_sem.at[2, h]).wait()
        rest = fin.at[h, many_f]
        local(rest, rest, q_sem.at[1, h]).wait()
        local(rest, rest, q_sem.at[0, h]).wait()


def run_layer(dims, rows, exps, tok, ids, probs):
    nz, nx, ny, fs, unit = dims
    ne, nf = nz * nx, 2 * ny
    gt, gs = nf * TOK, nf * CAP
    half, hidden, ups = nz * gs // 2, ne * unit, nz // 2
    chunk, hw, span = half // 2, fs // PIECES, unit * (fs // BLOCK)
    np = len(PARTS)
    vm = pl.BlockSpec(memory_space=pltpu.VMEM)
    hbm = pl.BlockSpec(memory_space=pltpu.HBM)
    anywhere = pl.BlockSpec(memory_space=pl.ANY)
    V = lambda *s: pltpu.VMEM(s, BF)
    W = lambda *s: pltpu.VMEM(s, F32)
    dma = lambda *s: pltpu.SemaphoreType.DMA(s)
    sums = [V(2, 2, ny, chunk, 2 * hidden)] * 4 + [V(2, 2, 2, chunk, 2 * hidden), V(2, 2, 2, chunk, hidden)]
    return pl.pallas_call(
        functools.partial(layer, dims),
        out_shape=(jax.ShapeDtypeStruct((2, 3, ne, unit, fs), BF), jax.ShapeDtypeStruct((TOK, nf * fs), BF)),
        in_specs=[hbm] * 5,
        out_specs=(vm, anywhere),
        scratch_shapes=[
            V(6, ne, unit, fs), pltpu.VMEM(exps.shape, jnp.int32), V(TOK, nf * fs), pltpu.VMEM(ids.shape, jnp.int32), W(*probs.shape), W(3, 2 * ne, span), W(3, 2 * ne, span), V(ne, 8, span), V(ne, 8, span),
            W(TOK, 128), W(PIECES, nz, gt, hw), V(nz, gt, fs), W(gt, 128), W(nz, 16, gt), W(nz, 16, gt),
            V(nx, 2, nz * gs, fs), V(2, nx, nz * gs, fs), V(2 * hidden, fs), V(PIECES, hidden, hw),
            *sums,
            V(2, 2, 2, ny, chunk, hidden), V(PIECES, 2, 2, nx, 2 * chunk, hw), V(PIECES, 2, 2, nx, 2 * chunk, hw),
            V(PIECES, 2, ups, gt, hw), V(PIECES, ups, gt, hw), V(PIECES, ups, gt, hw), V(PIECES, gt, hw),
            dma(6), dma(4), dma(np), dma(np), dma(np), dma(3), dma(3), dma(3), dma(2, 2, ups), dma(2, 2, ups), dma(3), dma(2, 2), dma(2),
            dma(2, 2, 2), dma(2, 2, 2, 4), dma(2, 2, 2), dma(2, 2, 2), dma(2, PIECES, 2, 2), dma(PIECES, 2, 2), dma(2, PIECES, ups), dma(2, PIECES, ups), dma(3, PIECES),
        ],
        compiler_params=pltpu.CompilerParams(collective_id=1, has_side_effects=True, vmem_limit_bytes=VMEM_LIMIT),
        name="layer",
    )(rows, exps, tok, ids, probs)


def body(dims, tokens, learner_rows, exponents, expert_ids, route_probs):
    nz, nx, ny, fs, unit = dims
    ne = nz * nx
    el, mixed = run_layer(dims, learner_rows.reshape(ne, 2, 3, unit, fs), exponents.transpose(1, 2, 3, 0), tokens, expert_ids.T, route_probs.T)
    return el.reshape(2, 3, ne * unit, fs), mixed


def make(mesh, dims):
    return jax.shard_map(
        functools.partial(body, dims),
        mesh=mesh,
        in_specs=(
            P(("fsdp", "expert"), None),
            P(None, None, "expert", "fsdp"),
            P(None, None, "expert", "fsdp"),
            P(("fsdp", "expert"), None),
            P(("fsdp", "expert"), None),
        ),
        out_specs=(P("expert", None, None, "fsdp"), P(("fsdp", "expert"), None)),
        check_vma=False,
    )


def solution(mesh):
    return make(mesh, (8, 4, 4, 512, 24))
```

```python
import functools
import jax
import jax.numpy as jnp
from jax import lax
from jax.experimental import pallas as pl
from jax.experimental.pallas import tpu as pltpu
from jax.sharding import PartitionSpec as P

BLOCK = 32
CAP = 4
NEAR = 20
SLICES = ((0, 20, 32), (1, 1, 20), (1, 20, 32), (2, 1, 20), (2, 20, 32))
ROWS = ((0, 16), (16, 8))
VMEM_LIMIT = 47 * 1024 * 1024
TOK = 16
MESH = pl.DeviceIdType.MESH
BF, F32 = jnp.bfloat16, jnp.float32
PHASES = ((0, 0), (0, 1), (1, 0), (1, 1), (0, 2), (1, 2))
PIECES = 2
PARTS = tuple((2 * k + p, *ROWS[u], 0, PIECES) for k in range(2) for u in range(2) for p in range(2)) + tuple(
    (4 + k, 0, 24, h, 1) for h in range(PIECES) for k in range(2))


def loop(low, high, step):
    def one(i, c):
        step(i)
        return c

    lax.fori_loop(low, high, one, 0)


def layer(dims, rows, exps_in, tok_in, ids_in, probs_in, out, mixed,
          enc, exps, tok, ids_raw, probs_raw, inv_t, scl_t, s_out, s_in, meta, mix, xcol, m_all, m_send, m_col, sbuf, slots, wgu, wdn,
          pa, pb, ra, rb, rc, rl, hid, osend, orecv, pm, up_sum, dn_sum, fin,
          load_sem, in_sem, e_send, e_recv, e_own, sc_sem, t_sem, m_sem, zu_sem, zd_sem, zm_sem, x_sem,
          x_own, a_sem, b_sem, h_sem, i_sem, o_sem, o_own, pu_sem, pd_sem, q_sem):
    nz, nx, ny, fs, unit = dims
    ne, nf = nz * nx, 2 * ny
    nb = fs // BLOCK
    gt, gs = nf * TOK, nf * CAP
    half = nz * gs // 2
    hidden = ne * unit
    wide_half = fs // PIECES
    ring_half = fs // 2
    sizes = tuple(ne * n for _, n in ROWS)
    starts = (0, sizes[0])
    experts, span = 2 * ne, unit * nb
    ups, downs = nz // 2, (nz - 1) // 2
    ex, f = lax.axis_index("expert"), lax.axis_index("fsdp")
    z, x = ex // nx, lax.rem(ex, nx)
    y, core = f // 2, lax.rem(f, 2)
    mate = y * 2 + (1 - core)
    barrier = pltpu.get_barrier_semaphore()

    def to_expert(src, dst, send, recv, e):
        return pltpu.make_async_remote_copy(src_ref=src, dst_ref=dst, send_sem=send, recv_sem=recv,
                                            device_id={"expert": e}, device_id_type=MESH)

    def to_fsdp(src, dst, send, recv, g):
        return pltpu.make_async_remote_copy(src_ref=src, dst_ref=dst, send_sem=send, recv_sem=recv,
                                            device_id={"fsdp": g}, device_id_type=MESH)

    def local(src, dst, sem):
        return pltpu.make_async_copy(src, dst, sem)

    def at_z(d):
        return lax.rem(z + d + nz, nz)

    small = [local(src, dst, in_sem.at[i]) for i, (src, dst) in enumerate(
        ((ids_in, ids_raw), (probs_in, probs_raw), (exps_in, exps), (tok_in, tok)))]

    def greet_expert(j):
        pl.semaphore_signal(barrier, inc=1, device_id={"expert": lax.rem(ex + j, ne)}, device_id_type=MESH)

    def greet_fsdp(j):
        pl.semaphore_signal(barrier, inc=1, device_id={"fsdp": lax.rem(f + j, nf)}, device_id_type=MESH)

    loop(1, nf, greet_fsdp)
    loop(1, ne, greet_expert)
    for copy in small:
        copy.start()
    for ph, (k, p) in enumerate(PHASES):
        local(rows.at[:, k, p], enc.at[ph], load_sem.at[ph]).start()

    small[0].wait()
    small[1].wait()
    top = ids_raw.shape[0]
    widen_lanes = (lax.broadcasted_iota(jnp.int32, (TOK, 128), 0) == lax.broadcasted_iota(jnp.int32, (TOK, 128), 1)).astype(F32)
    ids = jnp.dot(ids_raw[...].astype(F32), widen_lanes, precision=lax.Precision.HIGHEST, preferred_element_type=F32)
    probs = probs_raw[...] / jnp.sum(probs_raw[...], axis=0, keepdims=True)
    share = jnp.dot(probs, widen_lanes, precision=lax.Precision.HIGHEST, preferred_element_type=F32)
    expert_of = lax.broadcasted_iota(jnp.int32, (experts, 128), 0).astype(F32)
    member = jnp.zeros((experts, 128), F32)
    weight = jnp.zeros((experts, 128), F32)
    for i in range(top):
        hit = expert_of == ids[i:i + 1]
        member = member + hit.astype(F32)
        weight = weight + jnp.where(hit, share[i:i + 1], 0.0)
    before = lax.broadcasted_iota(jnp.int32, (128, 128), 0) < lax.broadcasted_iota(jnp.int32, (128, 128), 1)
    code = member * (1.0 + jnp.dot(member.astype(BF), before.astype(BF), preferred_element_type=F32))
    row_list = []
    for i in range(8):
        own = slice(i * 2 * nx, (i + 1) * 2 * nx)
        for table in (code, weight):
            if i < nz:
                row_list.append(table[own])
                if 2 * nx < 8:
                    row_list.append(jnp.zeros((8 - 2 * nx, 128), F32))
            else:
                row_list.append(jnp.zeros((8, 128), F32))
    meta[...] = jnp.transpose(jnp.concatenate(row_list, axis=0))[:TOK]

    small[2].wait()
    for p in range(3):
        flat = exps[p].reshape(span, experts).astype(F32)
        if experts < 128:
            flat = jnp.concatenate([flat, jnp.zeros((span, 128 - experts), F32)], axis=1)
        turned = jnp.transpose(flat)[:experts]
        inv_t[p] = jnp.exp2(-turned).astype(BF).astype(F32)
        scl_t[p] = jnp.exp2(turned).astype(BF).astype(F32)

    def gather_scales(o):
        lines = [scl_t[p, pl.ds(o * 2 + k, 1), :] for k in range(2) for p in range(3)]
        s_out[o] = jnp.concatenate(lines + [jnp.zeros((2, span), F32)], axis=0).astype(BF)

    loop(0, ne, gather_scales)

    spread_row = lax.broadcasted_iota(jnp.int32, (unit, span), 0)
    spread_lane = lax.broadcasted_iota(jnp.int32, (unit, span), 1)
    diagonal = spread_lane // nb == spread_row

    def pick(at=0, width=None):
        width = width or fs
        lane = lax.broadcasted_iota(jnp.int32, (span, width), 0)
        feat = lax.broadcasted_iota(jnp.int32, (span, width), 1) + at
        return (lax.rem(lane, nb) == feat // BLOCK).astype(BF)

    per = min(8, ne)

    def encode(ph):
        local(rows.at[:, 0, 0], enc.at[ph], load_sem.at[ph]).wait()
        k, p = PHASES[ph]
        sel = pick()

        def step(i):
            lines = [jnp.where(diagonal, inv_t[p, pl.ds((i * per + u) * 2 + k, 1), :], 0.0) for u in range(per)]
            wide = jnp.dot(jnp.concatenate(lines, axis=0).astype(BF), sel, preferred_element_type=F32)
            for u in range(per):
                v = enc[ph, i * per + u].astype(F32) * wide[u * unit:(u + 1) * unit]
                v = jnp.minimum(jnp.maximum(v, -6.0), 6.0)
                a = jnp.abs(v)
                magic = jnp.where(a < 2.0, 6291456.0, jnp.where(a < 4.0, 12582912.0, 25165824.0))
                enc[ph, i * per + u] = ((v + magic) - magic).astype(BF)

        loop(0, ne // per, step)

    def zigzag(i):
        return lax.rem(ex + jnp.where(lax.rem(i, 2) == 1, (i + 1) // 2, ne - i // 2), ne)

    def part(n, ref, who):
        ph, row, count, lo, width = PARTS[n]
        mine = ref.at[ph] if ref is enc else ref.at[PHASES[ph][0], PHASES[ph][1]]
        return mine.at[who, pl.ds(row, count), pl.ds(lo * wide_half, width * wide_half)]

    def elements_some(n, low, high):
        def step(i):
            e = zigzag(i)
            to_expert(part(n, enc, e), part(n, out, ex), e_send.at[n], e_recv.at[n], e).start()

        loop(low, high, step)

    def elements_send(n):
        elements_some(n, 1, ne)
        local(part(n, enc, ex), part(n, out, ex), e_own.at[n]).start()

    def scales_send(i):
        e = zigzag(i)
        to_expert(s_out.at[e], s_in.at[ex], sc_sem.at[0], sc_sem.at[1], e).start()

    encode(0)
    encode(1)
    small[3].wait()
    pl.semaphore_wait(barrier, ne + nf - 2)

    def tok_send(j):
        g = lax.rem(f + j, nf)
        here = pl.ds(pl.multiple_of(f * TOK, TOK), TOK)
        to_fsdp(tok.at[:, pl.ds(pl.multiple_of(g * fs, fs), fs)], xcol.at[z, here], t_sem.at[0], t_sem.at[1], g).start()
        to_fsdp(meta, m_all.at[here], m_sem.at[0], m_sem.at[1], g).start()

    here = pl.ds(pl.multiple_of(f * TOK, TOK), TOK)
    loop(1, nf, tok_send)
    local(tok.at[:, pl.ds(pl.multiple_of(f * fs, fs), fs)], xcol.at[z, here], t_sem.at[2]).start()
    local(meta, m_all.at[here], m_sem.at[2]).start()
    near = NEAR if ups == 4 else 2
    elements_some(0, 1, near)
    local(part(0, enc, ex), part(0, out, ex), e_own.at[0]).start()

    many_f = pl.ds(0, (nf - 1) * TOK)
    local(xcol.at[z, many_f], xcol.at[z, many_f], t_sem.at[1]).wait()
    local(xcol.at[z, here], xcol.at[z, here], t_sem.at[2]).wait()

    def cut(h, g):
        return xcol.at[g, :, pl.ds(h * ring_half, ring_half)]

    def push_up(h, step):
        g = at_z(1 - step)
        to_expert(cut(h, g), cut(h, g), zu_sem.at[0, h, step - 1], zu_sem.at[1, h, step - 1], at_z(1) * nx + x).start()

    def push_down(h, step):
        g = at_z(step - 1)
        to_expert(cut(h, g), cut(h, g), zd_sem.at[0, h, step - 1], zd_sem.at[1, h, step - 1], at_z(-1) * nx + x).start()

    for h in range(2):
        push_up(h, 1)
        if downs:
            push_down(h, 1)
    local(m_all.at[many_f], m_all.at[many_f], m_sem.at[1]).wait()
    local(meta, m_all.at[here], m_sem.at[2]).wait()
    turned = jnp.transpose(m_all[...])
    m_send[...] = turned.reshape(128 // 16, 16, gt)[:nz]

    def table_send(j):
        to = lax.rem(z + j, nz)
        to_expert(m_send.at[to], m_col.at[z], zm_sem.at[0], zm_sem.at[1], to * nx + x).start()

    loop(1, nz, table_send)
    local(m_send.at[z], m_col.at[z], zm_sem.at[2]).start()
    many_z = pl.ds(0, nz - 1)

    block4 = (lax.broadcasted_iota(jnp.int32, (2 * nx, gt), 1) // TOK * CAP).astype(F32)
    slot_of = lax.broadcasted_iota(jnp.int32, (gs, gt), 0).astype(F32)

    def targets(g):
        code = m_col[g, 0:2 * nx]
        return jnp.where(code > 0.5, block4 + code - 1.0, -1.0)

    def compact(g):
        tgt = targets(g)
        hot = jnp.concatenate([(slot_of == tgt[j:j + 1]).astype(F32) for j in range(2 * nx)], axis=0).astype(BF)
        taken = jnp.dot(hot, xcol[g], preferred_element_type=F32).astype(BF)
        at = pl.ds(pl.multiple_of(g * gs, gs), gs)
        for j in range(2 * nx):
            sbuf[j // 2, j % 2, at, :] = taken[j * gs:(j + 1) * gs]
        for j in range(1, nx):
            to = lax.rem(x + j, nx)
            to_expert(sbuf.at[to, 0, at], slots.at[0, x, at], x_sem.at[0, 0], x_sem.at[1, 0], z * nx + to).start()

    local(m_send.at[z], m_col.at[z], zm_sem.at[2]).wait()
    compact(z)
    for step in range(1, ups + 1):
        for h in range(2):
            local(cut(0, 0), cut(0, 0), zu_sem.at[1, h, step - 1]).wait()
            if step < ups:
                push_up(h, step + 1)
            if step <= downs:
                local(cut(0, 0), cut(0, 0), zd_sem.at[1, h, step - 1]).wait()
                if step < downs:
                    push_down(h, step + 1)
        if step == 1:
            local(m_col.at[many_z], m_col.at[many_z], zm_sem.at[1]).wait()
        if step == max(ups - 1, 1):
            loop(1, ne, scales_send)
            local(s_out.at[ex], s_in.at[ex], sc_sem.at[2]).start()
        if ups == 4:
            elements_some(*SLICES[step - 1])
        compact(at_z(-step))
        if step <= downs:
            compact(at_z(step))

    local(sbuf.at[x, 0], slots.at[0, x], x_own.at[0]).start()
    if ups == 4:
        elements_some(*SLICES[4])
        for n in (1, 2):
            local(part(n, enc, ex), part(n, out, ex), e_own.at[n]).start()
    else:
        elements_some(0, near, ne)
        elements_send(1)
        elements_send(2)
    elements_send(3)
    encode(2)
    elements_send(4)
    for j in range(1, nx):
        to = lax.rem(x + j, nx)
        to_expert(sbuf.at[to, 1], slots.at[1, x], x_sem.at[0, 1], x_sem.at[1, 1], z * nx + to).start()
    local(sbuf.at[x, 1], slots.at[1, x], x_own.at[1]).start()
    for ph in range(3, 6):
        encode(ph)

    many_e = pl.ds(0, ne - 1)
    many_x = pl.ds(0, nx - 1)
    many_y = pl.ds(0, ny - 1)

    def elements_wait(n):
        own, all_in = part(n, out, ex), part(n, out, many_e)
        local(own, own, e_own.at[n]).wait()
        local(all_in, all_in, e_recv.at[n]).wait()

    def widen(n, dst, base):
        ph, row, count, lo, width = PARTS[n]
        k, p = PHASES[ph]
        cols = width * wide_half
        sel = pick(lo * wide_half, cols)

        def step(i):
            lines = [jnp.where(diagonal, s_in[i * per + u].astype(F32)[k * 3 + p:k * 3 + p + 1], 0.0)[row:row + count] for u in range(per)]
            wide = jnp.dot(jnp.concatenate(lines, axis=0).astype(BF), sel, preferred_element_type=F32)
            vals = [out[k, p, i * per + u, pl.ds(row, count), pl.ds(lo * wide_half, cols)].astype(F32) * wide[u * count:(u + 1) * count] for u in range(per)]
            if count < unit:
                at = pl.multiple_of(base + i * per * count, per * count)
                dst[pl.ds(at, per * count), :] = jnp.concatenate(vals, axis=0).astype(BF)
            else:
                for (r, m), start in zip(ROWS, starts):
                    at = pl.multiple_of(start + i * per * m, per * m)
                    dst[pl.ds(at, per * m), :] = jnp.concatenate([v[r:r + m] for v in vals], axis=0).astype(BF)

        loop(0, ne // per, step)

    def gate_up(k, u, dst, which):
        lhs = slots[k, :, pl.ds(pl.multiple_of(which * half, half), half), :].reshape(nx * half, fs)
        cols = min(256, sizes[u])

        def step(n):
            at = pl.multiple_of(2 * starts[u] + n * cols, cols)
            res = lax.dot_general(lhs, wgu[pl.ds(at, cols), :], (((1,), (1,)), ((), ())), preferred_element_type=F32)
            dst[k, :, :, pl.ds(at, cols)] = res.astype(BF).reshape(ny, half, cols)

        loop(0, 2 * sizes[u] // cols, step)

    def both(u):
        return pl.ds(2 * starts[u], 2 * sizes[u])

    def first_sums(k, u):
        if u == 0:
            local(slots.at[k, many_x], slots.at[k, many_x], x_sem.at[1, k]).wait()
            local(sbuf.at[x, k], slots.at[k, x], x_own.at[k]).wait()
        for p in range(2):
            elements_wait(4 * k + 2 * u + p)
            widen(4 * k + 2 * u + p, wgu, 2 * starts[u] + p * sizes[u])
        gate_up(k, u, pa, 1 - core)
        to_fsdp(pa.at[k, :, :, both(u)], ra.at[k, :, :, both(u)], a_sem.at[0, k, u], a_sem.at[1, k, u], mate).start()
        gate_up(k, u, pb, core)
        local(pa.at[k, :, :, both(u)], ra.at[k, :, :, both(u)], a_sem.at[1, k, u]).wait()
        for j in ((2, 1, 3, 0) if ny == 4 else (1, 0)):
            to = lax.rem(y + j, ny)
            rb[k, to, :, both(u)] = (pb[k, to, :, both(u)].astype(F32) + ra[k, to, :, both(u)].astype(F32)).astype(BF)
            if ny == 4 and j == 2:
                for d in range(2):
                    side = rb.at[k, to, :, pl.ds(2 * starts[u] + d * sizes[u], sizes[u])]
                    to_fsdp(side, passed(rl, k, u, d), b_sem.at[0, k, u, d], b_sem.at[1, k, u, d], beside(d)).start()
        if ny != 4:
            to_fsdp(rb.at[k, 1 - y, :, both(u)], rc.at[k, 0, :, both(u)], b_sem.at[0, k, u, 2], b_sem.at[1, k, u, 2], (1 - y) * 2 + core).start()

    def passed(ref, k, u, d):
        return ref.at[k, d, :, pl.ds(starts[u], sizes[u])]

    def beside(d):
        return lax.rem(y + (1 if d == 0 else ny - 1), ny) * 2 + core

    def relay(k, u):
        if ny != 4:
            return
        for d in range(2):
            local(passed(rl, k, u, d), passed(rl, k, u, d), b_sem.at[1, k, u, d]).wait()
            to = lax.rem(y + (1 if d == 0 else ny - 1), ny)
            side = pl.ds(2 * starts[u] + d * sizes[u], sizes[u])
            rb[k, to, :, side] = (rb[k, to, :, side].astype(F32) + rl[k, d, :, pl.ds(starts[u], sizes[u])].astype(F32)).astype(BF)
            to_fsdp(rb.at[k, to, :, both(u)], rc.at[k, d, :, both(u)], b_sem.at[0, k, u, 2 + d], b_sem.at[1, k, u, 2 + d], beside(d)).start()

    def units(u):
        return pl.ds(starts[u], sizes[u])

    def activate(k, u):
        total = rb[k, y, :, both(u)].astype(F32)
        for d in range(2 if ny == 4 else 1):
            local(rc.at[k, d, :, both(u)], rc.at[k, d, :, both(u)], b_sem.at[1, k, u, 2 + d]).wait()
            total = total + rc[k, d, :, both(u)].astype(F32)
        gate, up = total[:, :sizes[u]], total[:, sizes[u]:]
        hid[k, core, y, :, units(u)] = (gate / (1.0 + jnp.exp(-gate)) * up).astype(BF)
        for j in range(1, ny):
            to = lax.rem(y + j, ny)
            mine = hid.at[k, core, y, :, units(u)]
            to_fsdp(mine, mine, h_sem.at[0, k, u], h_sem.at[1, k, u], to * 2 + core).start()

    def forward(k, u):
        some = hid.at[k, 0, many_y, :, units(u)]
        local(some, some, h_sem.at[1, k, u]).wait()
        mine = hid.at[k, core, :, :, units(u)]
        to_fsdp(mine, mine, i_sem.at[0, k, u], i_sem.at[1, k, u], mate).start()

    def hidden_wait(k):
        for u in range(2):
            some = hid.at[k, 0, :, :, units(u)]
            local(some, some, i_sem.at[1, k, u]).wait()

    def down(k, h):
        for j in range(nx):
            to = lax.rem(x + 1 + j, nx)
            lhs = jnp.concatenate([hid[k, 0, to], hid[k, 1, to]], axis=0)
            osend[h, k, to] = jnp.dot(lhs, wdn[...], preferred_element_type=F32).astype(BF)
            if j < nx - 1:
                to_expert(osend.at[h, k, to], orecv.at[h, k, x], o_sem.at[0, h, k], o_sem.at[1, h, k], z * nx + to).start()
            else:
                local(osend.at[h, k, to], orecv.at[h, k, to], o_own.at[h, k]).start()

    def outputs_wait(h):
        for k in range(2):
            local(orecv.at[h, k, many_x], orecv.at[h, k, many_x], o_sem.at[1, h, k]).wait()
            local(osend.at[h, k, x], orecv.at[h, k, x], o_own.at[h, k]).wait()

    def blend(h, g):
        tgt = targets(g)
        share = m_col[g, 8:8 + 2 * nx]
        hot = jnp.concatenate([jnp.where(slot_of == tgt[i:i + 1], share[i:i + 1], 0.0) for i in range(2 * nx)], axis=0)
        hi = hot.astype(BF)
        lo = (hot - hi.astype(F32)).astype(BF)
        at = pl.ds(pl.multiple_of(g * gs, gs), gs)
        vals = jnp.concatenate([orecv[h, i % 2, i // 2, at, :] for i in range(2 * nx)], axis=0)
        rows_of = (((0,), (0,)), ((), ()))
        res = lax.dot_general(hi, vals, rows_of, preferred_element_type=F32)
        return res + lax.dot_general(lo, vals, rows_of, preferred_element_type=F32)

    def blend_rest(h):
        for d in range(nz):
            if d not in (ups, downs + 2):
                mix[h, d] = blend(h, at_z(d))

    def sum_up(h, step):
        val = mix[h, ups + 1 - step]
        if step > 1:
            local(up_sum.at[h, 0], up_sum.at[h, 0], pu_sem.at[1, h, step - 2]).wait()
            val = val + up_sum[h, step - 2].astype(F32)
        pm[h, 0, step - 1] = val.astype(BF)
        to_expert(pm.at[h, 0, step - 1], up_sum.at[h, step - 1], pu_sem.at[0, h, step - 1], pu_sem.at[1, h, step - 1], at_z(1) * nx + x).start()

    def sum_down(h, step):
        val = mix[h, nz + step - downs - 1]
        if step > 1:
            local(dn_sum.at[h, 0], dn_sum.at[h, 0], pd_sem.at[1, h, step - 2]).wait()
            val = val + dn_sum[h, step - 2].astype(F32)
        pm[h, 1, step - 1] = val.astype(BF)
        to_expert(pm.at[h, 1, step - 1], dn_sum.at[h, step - 1], pd_sem.at[0, h, step - 1], pd_sem.at[1, h, step - 1], at_z(-1) * nx + x).start()

    def ring(h, step):
        sum_up(h, step)
        if step <= downs:
            sum_down(h, step)

    def finish(h):
        val = mix[h, 0]
        local(up_sum.at[h, 0], up_sum.at[h, 0], pu_sem.at[1, h, ups - 1]).wait()
        val = val + up_sum[h, ups - 1].astype(F32)
        if downs:
            local(dn_sum.at[h, 0], dn_sum.at[h, 0], pd_sem.at[1, h, downs - 1]).wait()
            val = val + dn_sum[h, downs - 1].astype(F32)
        fin[h] = val.astype(BF)
        cols = pl.ds(pl.multiple_of(f * fs + h * wide_half, wide_half), wide_half)

        def fin_send(j):
            g = lax.rem(f + j, nf)
            to_fsdp(fin.at[h, pl.ds(pl.multiple_of(g * TOK, TOK), TOK)], mixed.at[:, cols], q_sem.at[0, h], q_sem.at[1, h], g).start()

        loop(1, nf, fin_send)
        local(fin.at[h, here], mixed.at[:, cols], q_sem.at[2, h]).start()

    local(s_in.at[many_e], s_in.at[many_e], sc_sem.at[1]).wait()
    local(s_out.at[ex], s_in.at[ex], sc_sem.at[2]).wait()

    def last(n, k, h):
        elements_wait(n)
        widen(n, wdn, 0)
        if h == 0:
            hidden_wait(k)
        down(k, h)

    def begin(h):
        outputs_wait(h)
        for d in (ups, downs + 2) if downs else (ups,):
            mix[h, d] = blend(h, at_z(d))
        ring(h, 1)
        blend_rest(h)

    first_sums(0, 0)
    elements_send(5)
    first_sums(0, 1)
    relay(0, 0)
    elements_send(6)
    elements_send(7)
    relay(0, 1)
    activate(0, 0)
    activate(0, 1)
    elements_send(8)
    first_sums(1, 0)
    forward(0, 0)
    forward(0, 1)
    elements_send(9)
    relay(1, 0)
    first_sums(1, 1)
    elements_send(10)
    elements_send(11)
    activate(1, 0)
    relay(1, 1)
    last(8, 0, 0)
    activate(1, 1)
    forward(1, 0)
    forward(1, 1)
    last(9, 1, 0)
    last(10, 0, 1)
    begin(0)
    last(11, 1, 1)
    for step in range(2, ups):
        ring(0, step)
    begin(1)
    if ups > 1:
        ring(0, ups)
    for step in range(2, ups + 1):
        ring(1, step)
        if step == min(3, ups):
            finish(0)
    if ups == 1:
        finish(0)
    finish(1)

    for n in range(len(PARTS)):
        out_n = part(n, enc, many_e)
        local(out_n, out_n, e_send.at[n]).wait()
    local(s_in.at[many_e], s_in.at[many_e], sc_sem.at[0]).wait()
    local(xcol.at[z, many_f], xcol.at[z, many_f], t_sem.at[0]).wait()
    local(m_all.at[many_f], m_all.at[many_f], m_sem.at[0]).wait()
    for h in range(2):
        for step in range(ups):
            local(cut(0, 0), cut(0, 0), zu_sem.at[0, h, step]).wait()
        for step in range(downs):
            local(cut(0, 0), cut(0, 0), zd_sem.at[0, h, step]).wait()
    local(m_col.at[many_z], m_col.at[many_z], zm_sem.at[0]).wait()
    for k in range(2):
        local(slots.at[k, many_x], slots.at[k, many_x], x_sem.at[0, k]).wait()
        for u in range(2):
            local(pa.at[k, :, :, both(u)], pa.at[k, :, :, both(u)], a_sem.at[0, k, u]).wait()
            for d in range(2 if ny == 4 else 1):
                local(rc.at[k, d, :, both(u)], rc.at[k, d, :, both(u)], b_sem.at[0, k, u, 2 + d]).wait()
                if ny == 4:
                    local(passed(rl, k, u, d), passed(rl, k, u, d), b_sem.at[0, k, u, d]).wait()
            some, full = hid.at[k, 0, many_y, :, units(u)], hid.at[k, 0, :, :, units(u)]
            local(some, some, h_sem.at[0, k, u]).wait()
            local(full, full, i_sem.at[0, k, u]).wait()
    for h in range(PIECES):
        for k in range(2):
            local(orecv.at[h, k, many_x], orecv.at[h, k, many_x], o_sem.at[0, h, k]).wait()
        for step in range(ups):
            local(up_sum.at[h, 0], up_sum.at[h, 0], pu_sem.at[0, h, step]).wait()
        for step in range(downs):
            local(dn_sum.at[h, 0], dn_sum.at[h, 0], pd_sem.at[0, h, step]).wait()
        mine = fin.at[h, here]
        local(mine, mine, q_sem.at[2, h]).wait()
        rest = fin.at[h, many_f]
        local(rest, rest, q_sem.at[1, h]).wait()
        local(rest, rest, q_sem.at[0, h]).wait()


def run_layer(dims, rows, exps, tok, ids, probs):
    nz, nx, ny, fs, unit = dims
    ne, nf = nz * nx, 2 * ny
    gt, gs = nf * TOK, nf * CAP
    half, hidden, ups = nz * gs // 2, ne * unit, nz // 2
    hw, span = fs // PIECES, unit * (fs // BLOCK)
    np = len(PARTS)
    vm = pl.BlockSpec(memory_space=pltpu.VMEM)
    hbm = pl.BlockSpec(memory_space=pltpu.HBM)
    anywhere = pl.BlockSpec(memory_space=pl.ANY)
    V = lambda *s: pltpu.VMEM(s, BF)
    W = lambda *s: pltpu.VMEM(s, F32)
    dma = lambda *s: pltpu.SemaphoreType.DMA(s)
    sums = [V(2, ny, half, 2 * hidden)] * 4 + [V(2, 2, half, 2 * hidden), V(2, 2, half, hidden)]
    return pl.pallas_call(
        functools.partial(layer, dims),
        out_shape=(jax.ShapeDtypeStruct((2, 3, ne, unit, fs), BF), jax.ShapeDtypeStruct((TOK, nf * fs), BF)),
        in_specs=[hbm] * 5,
        out_specs=(vm, anywhere),
        scratch_shapes=[
            V(6, ne, unit, fs), pltpu.VMEM(exps.shape, jnp.int32), V(TOK, nf * fs), pltpu.VMEM(ids.shape, jnp.int32), W(*probs.shape), W(3, 2 * ne, span), W(3, 2 * ne, span), V(ne, 8, span), V(ne, 8, span),
            W(TOK, 128), W(PIECES, nz, gt, hw), V(nz, gt, fs), W(gt, 128), W(nz, 16, gt), W(nz, 16, gt),
            V(nx, 2, nz * gs, fs), V(2, nx, nz * gs, fs), V(2 * hidden, fs), V(hidden, hw),
            *sums,
            V(2, 2, ny, half, hidden), V(PIECES, 2, nx, 2 * half, hw), V(PIECES, 2, nx, 2 * half, hw),
            V(PIECES, 2, ups, gt, hw), V(PIECES, ups, gt, hw), V(PIECES, ups, gt, hw), V(PIECES, gt, hw),
            dma(6), dma(4), dma(np), dma(np), dma(np), dma(3), dma(3), dma(3), dma(2, 2, ups), dma(2, 2, ups), dma(3), dma(2, 2), dma(2),
            dma(2, 2, 2), dma(2, 2, 2, 4), dma(2, 2, 2), dma(2, 2, 2), dma(2, PIECES, 2), dma(PIECES, 2), dma(2, PIECES, ups), dma(2, PIECES, ups), dma(3, PIECES),
        ],
        compiler_params=pltpu.CompilerParams(collective_id=1, has_side_effects=True, vmem_limit_bytes=VMEM_LIMIT),
        name="layer",
    )(rows, exps, tok, ids, probs)


def body(dims, tokens, learner_rows, exponents, expert_ids, route_probs):
    nz, nx, ny, fs, unit = dims
    ne = nz * nx
    el, mixed = run_layer(dims, learner_rows.reshape(ne, 2, 3, unit, fs), exponents.transpose(1, 2, 3, 0), tokens, expert_ids.T, route_probs.T)
    return el.reshape(2, 3, ne * unit, fs), mixed


def make(mesh, dims):
    return jax.shard_map(
        functools.partial(body, dims),
        mesh=mesh,
        in_specs=(
            P(("fsdp", "expert"), None),
            P(None, None, "expert", "fsdp"),
            P(None, None, "expert", "fsdp"),
            P(("fsdp", "expert"), None),
            P(("fsdp", "expert"), None),
        ),
        out_specs=(P("expert", None, None, "fsdp"), P(("fsdp", "expert"), None)),
        check_vma=False,
    )


def solution(mesh):
    return make(mesh, (8, 4, 4, 512, 24))
```

```python
import functools
import jax
import jax.numpy as jnp
from jax import lax
from jax.experimental import pallas as pl
from jax.experimental.pallas import tpu as pltpu
from jax.sharding import PartitionSpec as P

BLOCK = 32
CAP = 4
NEAR = 20
SLICES = ((0, 20, 26), (0, 26, 32), (1, 1, 16), (1, 16, 24), (1, 24, 32))
VMEM_LIMIT = 47 * 1024 * 1024
TOK = 16
MESH = pl.DeviceIdType.MESH
BF, F32 = jnp.bfloat16, jnp.float32
PHASES = ((0, 0), (0, 1), (1, 0), (1, 1), (0, 2), (1, 2))
PIECES = 2
PARTS = tuple((ph, 0, PIECES) for ph in range(4)) + tuple((ph, h, 1) for ph in (4, 5) for h in range(PIECES))


def loop(low, high, step):
    def one(i, c):
        step(i)
        return c

    lax.fori_loop(low, high, one, 0)


def layer(dims, rows, exps_in, tok_in, ids_in, probs_in, out, mixed,
          enc, exps, tok, ids_raw, probs_raw, inv_t, scl_t, s_out, s_in, meta, mix, xcol, m_all, m_send, m_col, sbuf, slots, wgu, wdn,
          pa, pb, ra, rb, rc, rl, hid, osend, orecv, pm, up_sum, dn_sum, fin,
          load_sem, in_sem, e_send, e_recv, e_own, sc_sem, t_sem, m_sem, zu_sem, zd_sem, zm_sem, x_sem,
          x_own, a_sem, b_sem, h_sem, i_sem, o_sem, o_own, pu_sem, pd_sem, q_sem):
    nz, nx, ny, fs, unit = dims
    ne, nf = nz * nx, 2 * ny
    nb = fs // BLOCK
    gt, gs = nf * TOK, nf * CAP
    half = nz * gs // 2
    hidden = ne * unit
    wide_half = fs // PIECES
    ring_half = fs // 2
    chunk = half // 2
    experts, span = 2 * ne, unit * nb
    ups, downs = nz // 2, (nz - 1) // 2
    ex, f = lax.axis_index("expert"), lax.axis_index("fsdp")
    z, x = ex // nx, lax.rem(ex, nx)
    y, core = f // 2, lax.rem(f, 2)
    mate = y * 2 + (1 - core)
    barrier = pltpu.get_barrier_semaphore()

    def to_expert(src, dst, send, recv, e):
        return pltpu.make_async_remote_copy(src_ref=src, dst_ref=dst, send_sem=send, recv_sem=recv,
                                            device_id={"expert": e}, device_id_type=MESH)

    def to_fsdp(src, dst, send, recv, g):
        return pltpu.make_async_remote_copy(src_ref=src, dst_ref=dst, send_sem=send, recv_sem=recv,
                                            device_id={"fsdp": g}, device_id_type=MESH)

    def local(src, dst, sem):
        return pltpu.make_async_copy(src, dst, sem)

    def at_z(d):
        return lax.rem(z + d + nz, nz)

    small = [local(src, dst, in_sem.at[i]) for i, (src, dst) in enumerate(
        ((ids_in, ids_raw), (probs_in, probs_raw), (exps_in, exps), (tok_in, tok)))]

    def greet_expert(j):
        pl.semaphore_signal(barrier, inc=1, device_id={"expert": lax.rem(ex + j, ne)}, device_id_type=MESH)

    def greet_fsdp(j):
        pl.semaphore_signal(barrier, inc=1, device_id={"fsdp": lax.rem(f + j, nf)}, device_id_type=MESH)

    loop(1, nf, greet_fsdp)
    loop(1, ne, greet_expert)
    for copy in small:
        copy.start()
    for ph, (k, p) in enumerate(PHASES):
        local(rows.at[:, k, p], enc.at[ph], load_sem.at[ph]).start()

    small[0].wait()
    small[1].wait()
    top = ids_raw.shape[0]
    widen_lanes = (lax.broadcasted_iota(jnp.int32, (TOK, 128), 0) == lax.broadcasted_iota(jnp.int32, (TOK, 128), 1)).astype(F32)
    ids = jnp.dot(ids_raw[...].astype(F32), widen_lanes, precision=lax.Precision.HIGHEST, preferred_element_type=F32)
    probs = probs_raw[...] / jnp.sum(probs_raw[...], axis=0, keepdims=True)
    share = jnp.dot(probs, widen_lanes, precision=lax.Precision.HIGHEST, preferred_element_type=F32)
    expert_of = lax.broadcasted_iota(jnp.int32, (experts, 128), 0).astype(F32)
    member = jnp.zeros((experts, 128), F32)
    weight = jnp.zeros((experts, 128), F32)
    for i in range(top):
        hit = expert_of == ids[i:i + 1]
        member = member + hit.astype(F32)
        weight = weight + jnp.where(hit, share[i:i + 1], 0.0)
    before = lax.broadcasted_iota(jnp.int32, (128, 128), 0) < lax.broadcasted_iota(jnp.int32, (128, 128), 1)
    code = member * (1.0 + jnp.dot(member.astype(BF), before.astype(BF), preferred_element_type=F32))
    row_list = []
    for i in range(8):
        own = slice(i * 2 * nx, (i + 1) * 2 * nx)
        for table in (code, weight):
            if i < nz:
                row_list.append(table[own])
                if 2 * nx < 8:
                    row_list.append(jnp.zeros((8 - 2 * nx, 128), F32))
            else:
                row_list.append(jnp.zeros((8, 128), F32))
    meta[...] = jnp.transpose(jnp.concatenate(row_list, axis=0))[:TOK]

    small[2].wait()
    for p in range(3):
        flat = exps[p].reshape(span, experts).astype(F32)
        if experts < 128:
            flat = jnp.concatenate([flat, jnp.zeros((span, 128 - experts), F32)], axis=1)
        turned = jnp.transpose(flat)[:experts]
        inv_t[p] = jnp.exp2(-turned).astype(BF).astype(F32)
        scl_t[p] = jnp.exp2(turned).astype(BF).astype(F32)

    def gather_scales(o):
        lines = [scl_t[p, pl.ds(o * 2 + k, 1), :] for k in range(2) for p in range(3)]
        s_out[o] = jnp.concatenate(lines + [jnp.zeros((2, span), F32)], axis=0).astype(BF)

    loop(0, ne, gather_scales)

    spread_row = lax.broadcasted_iota(jnp.int32, (unit, span), 0)
    spread_lane = lax.broadcasted_iota(jnp.int32, (unit, span), 1)
    diagonal = spread_lane // nb == spread_row

    def pick(at=0, width=None):
        width = width or fs
        lane = lax.broadcasted_iota(jnp.int32, (span, width), 0)
        feat = lax.broadcasted_iota(jnp.int32, (span, width), 1) + at
        return (lax.rem(lane, nb) == feat // BLOCK).astype(BF)

    per = min(8, ne)

    def encode(ph):
        local(rows.at[:, 0, 0], enc.at[ph], load_sem.at[ph]).wait()
        k, p = PHASES[ph]
        sel = pick()

        def step(i):
            lines = [jnp.where(diagonal, inv_t[p, pl.ds((i * per + u) * 2 + k, 1), :], 0.0) for u in range(per)]
            wide = jnp.dot(jnp.concatenate(lines, axis=0).astype(BF), sel, preferred_element_type=F32)
            for u in range(per):
                v = enc[ph, i * per + u].astype(F32) * wide[u * unit:(u + 1) * unit]
                v = jnp.minimum(jnp.maximum(v, -6.0), 6.0)
                a = jnp.abs(v)
                magic = jnp.where(a < 2.0, 6291456.0, jnp.where(a < 4.0, 12582912.0, 25165824.0))
                enc[ph, i * per + u] = ((v + magic) - magic).astype(BF)

        loop(0, ne // per, step)

    def zigzag(i):
        return lax.rem(ex + jnp.where(lax.rem(i, 2) == 1, (i + 1) // 2, ne - i // 2), ne)

    def part(n, ref, who):
        ph, lo, width = PARTS[n]
        mine = ref.at[ph] if ref is enc else ref.at[PHASES[ph][0], PHASES[ph][1]]
        return mine.at[who] if width == PIECES else mine.at[who, :, pl.ds(lo * wide_half, wide_half)]

    def elements_some(n, low, high):
        def step(i):
            e = zigzag(i)
            to_expert(part(n, enc, e), part(n, out, ex), e_send.at[n], e_recv.at[n], e).start()

        loop(low, high, step)

    def elements_send(n):
        elements_some(n, 1, ne)
        local(part(n, enc, ex), part(n, out, ex), e_own.at[n]).start()

    def scales_send(i):
        e = zigzag(i)
        to_expert(s_out.at[e], s_in.at[ex], sc_sem.at[0], sc_sem.at[1], e).start()

    encode(0)
    encode(1)
    small[3].wait()
    pl.semaphore_wait(barrier, ne + nf - 2)

    def tok_send(j):
        g = lax.rem(f + j, nf)
        here = pl.ds(pl.multiple_of(f * TOK, TOK), TOK)
        to_fsdp(tok.at[:, pl.ds(pl.multiple_of(g * fs, fs), fs)], xcol.at[z, here], t_sem.at[0], t_sem.at[1], g).start()
        to_fsdp(meta, m_all.at[here], m_sem.at[0], m_sem.at[1], g).start()

    here = pl.ds(pl.multiple_of(f * TOK, TOK), TOK)
    loop(1, nf, tok_send)
    local(tok.at[:, pl.ds(pl.multiple_of(f * fs, fs), fs)], xcol.at[z, here], t_sem.at[2]).start()
    local(meta, m_all.at[here], m_sem.at[2]).start()
    near = NEAR if ups == 4 else 2
    elements_some(0, 1, near)
    local(part(0, enc, ex), part(0, out, ex), e_own.at[0]).start()

    many_f = pl.ds(0, (nf - 1) * TOK)
    local(xcol.at[z, many_f], xcol.at[z, many_f], t_sem.at[1]).wait()
    local(xcol.at[z, here], xcol.at[z, here], t_sem.at[2]).wait()

    def cut(h, g):
        return xcol.at[g, :, pl.ds(h * ring_half, ring_half)]

    def push_up(h, step):
        g = at_z(1 - step)
        to_expert(cut(h, g), cut(h, g), zu_sem.at[0, h, step - 1], zu_sem.at[1, h, step - 1], at_z(1) * nx + x).start()

    def push_down(h, step):
        g = at_z(step - 1)
        to_expert(cut(h, g), cut(h, g), zd_sem.at[0, h, step - 1], zd_sem.at[1, h, step - 1], at_z(-1) * nx + x).start()

    for h in range(2):
        push_up(h, 1)
        if downs:
            push_down(h, 1)
    local(m_all.at[many_f], m_all.at[many_f], m_sem.at[1]).wait()
    local(meta, m_all.at[here], m_sem.at[2]).wait()
    turned = jnp.transpose(m_all[...])
    m_send[...] = turned.reshape(128 // 16, 16, gt)[:nz]

    def table_send(j):
        to = lax.rem(z + j, nz)
        to_expert(m_send.at[to], m_col.at[z], zm_sem.at[0], zm_sem.at[1], to * nx + x).start()

    loop(1, nz, table_send)
    local(m_send.at[z], m_col.at[z], zm_sem.at[2]).start()
    many_z = pl.ds(0, nz - 1)

    block4 = (lax.broadcasted_iota(jnp.int32, (2 * nx, gt), 1) // TOK * CAP).astype(F32)
    slot_of = lax.broadcasted_iota(jnp.int32, (gs, gt), 0).astype(F32)

    def targets(g):
        code = m_col[g, 0:2 * nx]
        return jnp.where(code > 0.5, block4 + code - 1.0, -1.0)

    def compact(g):
        tgt = targets(g)
        hot = jnp.concatenate([(slot_of == tgt[j:j + 1]).astype(F32) for j in range(2 * nx)], axis=0).astype(BF)
        taken = jnp.dot(hot, xcol[g], preferred_element_type=F32).astype(BF)
        at = pl.ds(pl.multiple_of(g * gs, gs), gs)
        for j in range(2 * nx):
            sbuf[j // 2, j % 2, at, :] = taken[j * gs:(j + 1) * gs]
        for j in range(1, nx):
            to = lax.rem(x + j, nx)
            to_expert(sbuf.at[to, 0, at], slots.at[0, x, at], x_sem.at[0, 0], x_sem.at[1, 0], z * nx + to).start()

    local(m_send.at[z], m_col.at[z], zm_sem.at[2]).wait()
    compact(z)
    for step in range(1, ups + 1):
        for h in range(2):
            local(cut(0, 0), cut(0, 0), zu_sem.at[1, h, step - 1]).wait()
            if step < ups:
                push_up(h, step + 1)
            if step <= downs:
                local(cut(0, 0), cut(0, 0), zd_sem.at[1, h, step - 1]).wait()
                if step < downs:
                    push_down(h, step + 1)
        if step == 1:
            local(m_col.at[many_z], m_col.at[many_z], zm_sem.at[1]).wait()
        if step == max(ups - 1, 1):
            loop(1, ne, scales_send)
            local(s_out.at[ex], s_in.at[ex], sc_sem.at[2]).start()
        if ups == 4:
            elements_some(*SLICES[step - 1])
        compact(at_z(-step))
        if step <= downs:
            compact(at_z(step))

    local(sbuf.at[x, 0], slots.at[0, x], x_own.at[0]).start()
    if ups == 4:
        elements_some(*SLICES[4])
        local(part(1, enc, ex), part(1, out, ex), e_own.at[1]).start()
    else:
        elements_some(0, near, ne)
        elements_send(1)
    encode(2)
    elements_send(2)
    for j in range(1, nx):
        to = lax.rem(x + j, nx)
        to_expert(sbuf.at[to, 1], slots.at[1, x], x_sem.at[0, 1], x_sem.at[1, 1], z * nx + to).start()
    local(sbuf.at[x, 1], slots.at[1, x], x_own.at[1]).start()
    for ph in range(3, 6):
        encode(ph)

    many_e = pl.ds(0, ne - 1)
    many_x = pl.ds(0, nx - 1)
    many_y = pl.ds(0, ny - 1)

    def elements_wait(n):
        own, all_in = part(n, out, ex), part(n, out, many_e)
        local(own, own, e_own.at[n]).wait()
        local(all_in, all_in, e_recv.at[n]).wait()

    def widen(n, dst, base):
        ph, lo, width = PARTS[n]
        k, p = PHASES[ph]
        cols = width * wide_half
        sel = pick(lo * wide_half, cols)

        def step(i):
            at = pl.multiple_of(i * per * unit, per * unit)
            lines = [jnp.where(diagonal, s_in[i * per + u].astype(F32)[k * 3 + p:k * 3 + p + 1], 0.0) for u in range(per)]
            wide = jnp.dot(jnp.concatenate(lines, axis=0).astype(BF), sel, preferred_element_type=F32)
            vals = [out[k, p, i * per + u, :, pl.ds(lo * wide_half, cols)].astype(F32) * wide[u * unit:(u + 1) * unit] for u in range(per)]
            dst[pl.ds(base + at, per * unit), :] = jnp.concatenate(vals, axis=0).astype(BF)

        loop(0, ne // per, step)

    cols = min(256, hidden)

    def gate_up(k, c, dst, which, base):
        lhs = slots[k, :, pl.ds(pl.multiple_of(which * half + c * chunk, chunk), chunk), :].reshape(nx * chunk, fs)

        def step(n):
            at = pl.multiple_of(base + n * cols, cols)
            res = lax.dot_general(lhs, wgu[pl.ds(at, cols), :], (((1,), (1,)), ((), ())), preferred_element_type=F32)
            dst[k, c, :, :, pl.ds(at, cols)] = res.astype(BF).reshape(ny, chunk, cols)

        loop(0, hidden // cols, step)

    def gates(k):
        elements_wait(2 * k)
        widen(2 * k, wgu, 0)
        local(slots.at[k, many_x], slots.at[k, many_x], x_sem.at[1, k]).wait()
        local(sbuf.at[x, k], slots.at[k, x], x_own.at[k]).wait()
        for c in range(2):
            gate_up(k, c, pa, 1 - core, 0)
            gate_up(k, c, pb, core, 0)

    def first_sums(k):
        elements_wait(2 * k + 1)
        widen(2 * k + 1, wgu, hidden)
        def collect(c):
            local(pa.at[k, c], ra.at[k, c], a_sem.at[1, k, c]).wait()
            for j in ((2, 1, 3, 0) if ny == 4 else (1, 0)):
                to = lax.rem(y + j, ny)
                rb[k, c, to] = (pb[k, c, to].astype(F32) + ra[k, c, to].astype(F32)).astype(BF)
                if ny == 4 and j == 2:
                    for d in range(2):
                        side = rb.at[k, c, to, :, pl.ds(d * hidden, hidden)]
                        to_fsdp(side, rl.at[k, c, d], b_sem.at[0, k, c, d], b_sem.at[1, k, c, d], beside(d)).start()
            if ny != 4:
                to_fsdp(rb.at[k, c, 1 - y], rc.at[k, c, 0], b_sem.at[0, k, c, 2], b_sem.at[1, k, c, 2], (1 - y) * 2 + core).start()

        for c in range(2):
            gate_up(k, c, pa, 1 - core, hidden)
            to_fsdp(pa.at[k, c], ra.at[k, c], a_sem.at[0, k, c], a_sem.at[1, k, c], mate).start()
            gate_up(k, c, pb, core, hidden)
            if c == 0:
                collect(0)
        collect(1)

    def beside(d):
        return lax.rem(y + (1 if d == 0 else ny - 1), ny) * 2 + core

    def relay(k, c):
        if ny != 4:
            return
        for d in range(2):
            local(rl.at[k, c, d], rl.at[k, c, d], b_sem.at[1, k, c, d]).wait()
            to = lax.rem(y + (1 if d == 0 else ny - 1), ny)
            side = pl.ds(d * hidden, hidden)
            rb[k, c, to, :, side] = (rb[k, c, to, :, side].astype(F32) + rl[k, c, d].astype(F32)).astype(BF)
            to_fsdp(rb.at[k, c, to], rc.at[k, c, d], b_sem.at[0, k, c, 2 + d], b_sem.at[1, k, c, 2 + d], beside(d)).start()

    def activate(k, c):
        total = rb[k, c, y].astype(F32)
        for d in range(2 if ny == 4 else 1):
            local(rc.at[k, c, d], rc.at[k, c, d], b_sem.at[1, k, c, 2 + d]).wait()
            total = total + rc[k, c, d].astype(F32)
        gate, up = total[:, :hidden], total[:, hidden:]
        hid[k, c, core, y] = (gate / (1.0 + jnp.exp(-gate)) * up).astype(BF)
        for j in range(1, ny):
            to = lax.rem(y + j, ny)
            to_fsdp(hid.at[k, c, core, y], hid.at[k, c, core, y], h_sem.at[0, k, c], h_sem.at[1, k, c], to * 2 + core).start()

    def forward(k, c):
        local(hid.at[k, c, 0, many_y], hid.at[k, c, 0, many_y], h_sem.at[1, k, c]).wait()
        to_fsdp(hid.at[k, c, core], hid.at[k, c, core], i_sem.at[0, k, c], i_sem.at[1, k, c], mate).start()

    def hidden_wait(k, c):
        local(hid.at[k, c, 0], hid.at[k, c, 0], i_sem.at[1, k, c]).wait()

    def down(k, h, c):
        for j in range(nx):
            to = lax.rem(x + 1 + j, nx)
            lhs = jnp.concatenate([hid[k, c, 0, to], hid[k, c, 1, to]], axis=0)
            osend[h, k, c, to] = jnp.dot(lhs, wdn[h], preferred_element_type=F32).astype(BF)
            if j < nx - 1:
                to_expert(osend.at[h, k, c, to], orecv.at[h, k, c, x], o_sem.at[0, h, k, c], o_sem.at[1, h, k, c], z * nx + to).start()
            else:
                local(osend.at[h, k, c, to], orecv.at[h, k, c, to], o_own.at[h, k, c]).start()

    def outputs_wait(h):
        for k in range(2):
            for c in range(2):
                local(orecv.at[h, k, c, many_x], orecv.at[h, k, c, many_x], o_sem.at[1, h, k, c]).wait()
                local(osend.at[h, k, c, x], orecv.at[h, k, c, x], o_own.at[h, k, c]).wait()

    def blend(h, g):
        tgt = targets(g)
        share = m_col[g, 8:8 + 2 * nx]
        hot = jnp.concatenate([jnp.where(slot_of == tgt[i:i + 1], share[i:i + 1], 0.0) for i in range(2 * nx)], axis=0)
        hi = hot.astype(BF)
        lo = (hot - hi.astype(F32)).astype(BF)
        which, inside = g // (nz // 2), lax.rem(g, nz // 2) * gs
        c, spot = inside // chunk, lax.rem(inside, chunk)
        at = pl.ds(pl.multiple_of(which * chunk + spot, gs), gs)
        vals = jnp.concatenate([orecv[h, i % 2, c, i // 2, at, :] for i in range(2 * nx)], axis=0)
        both = (((0,), (0,)), ((), ()))
        res = lax.dot_general(hi, vals, both, preferred_element_type=F32)
        return res + lax.dot_general(lo, vals, both, preferred_element_type=F32)

    def blend_rest(h):
        for d in range(nz):
            if d not in (ups, downs + 2):
                mix[h, d] = blend(h, at_z(d))

    def sum_up(h, step):
        val = mix[h, ups + 1 - step]
        if step > 1:
            local(up_sum.at[h, 0], up_sum.at[h, 0], pu_sem.at[1, h, step - 2]).wait()
            val = val + up_sum[h, step - 2].astype(F32)
        pm[h, 0, step - 1] = val.astype(BF)
        to_expert(pm.at[h, 0, step - 1], up_sum.at[h, step - 1], pu_sem.at[0, h, step - 1], pu_sem.at[1, h, step - 1], at_z(1) * nx + x).start()

    def sum_down(h, step):
        val = mix[h, nz + step - downs - 1]
        if step > 1:
            local(dn_sum.at[h, 0], dn_sum.at[h, 0], pd_sem.at[1, h, step - 2]).wait()
            val = val + dn_sum[h, step - 2].astype(F32)
        pm[h, 1, step - 1] = val.astype(BF)
        to_expert(pm.at[h, 1, step - 1], dn_sum.at[h, step - 1], pd_sem.at[0, h, step - 1], pd_sem.at[1, h, step - 1], at_z(-1) * nx + x).start()

    def ring(h, step):
        sum_up(h, step)
        if step <= downs:
            sum_down(h, step)

    def finish(h):
        val = mix[h, 0]
        local(up_sum.at[h, 0], up_sum.at[h, 0], pu_sem.at[1, h, ups - 1]).wait()
        val = val + up_sum[h, ups - 1].astype(F32)
        if downs:
            local(dn_sum.at[h, 0], dn_sum.at[h, 0], pd_sem.at[1, h, downs - 1]).wait()
            val = val + dn_sum[h, downs - 1].astype(F32)
        fin[h] = val.astype(BF)
        cols = pl.ds(pl.multiple_of(f * fs + h * wide_half, wide_half), wide_half)

        def fin_send(j):
            g = lax.rem(f + j, nf)
            to_fsdp(fin.at[h, pl.ds(pl.multiple_of(g * TOK, TOK), TOK)], mixed.at[:, cols], q_sem.at[0, h], q_sem.at[1, h], g).start()

        loop(1, nf, fin_send)
        local(fin.at[h, here], mixed.at[:, cols], q_sem.at[2, h]).start()

    local(s_in.at[many_e], s_in.at[many_e], sc_sem.at[1]).wait()
    local(s_out.at[ex], s_in.at[ex], sc_sem.at[2]).wait()

    gates(0)
    elements_send(3)
    first_sums(0)
    relay(0, 0)
    relay(0, 1)
    gates(1)
    for n in range(4, 4 + PIECES):
        elements_send(n)
    activate(0, 0)
    activate(0, 1)
    first_sums(1)
    for n in range(4 + PIECES, len(PARTS)):
        elements_send(n)
    for c in range(2):
        forward(0, c)
    relay(1, 0)
    relay(1, 1)
    for h in range(PIECES):
        elements_wait(4 + h)
        widen(4 + h, wdn.at[h], 0)
        for c in range(2):
            if h == 0:
                hidden_wait(0, c)
            down(0, h, c)
        if h == 0:
            activate(1, 0)
    activate(1, 1)
    forward(1, 0)
    for h in range(PIECES):
        elements_wait(4 + PIECES + h)
        widen(4 + PIECES + h, wdn.at[h], 0)
        if h == 0:
            hidden_wait(1, 0)
        down(1, h, 0)
        if h == 0:
            forward(1, 1)
            hidden_wait(1, 1)
        down(1, h, 1)
    for t in range(PIECES + ups):
        for h in range(PIECES):
            step = t - h + 1
            if step == 1:
                outputs_wait(h)
                for d in (ups, downs + 2) if downs else (ups,):
                    mix[h, d] = blend(h, at_z(d))
            if 1 <= step <= ups:
                ring(h, step)
            if step == 1:
                blend_rest(h)
            if step == ups + 1:
                finish(h)

    for n in range(len(PARTS)):
        out_n = part(n, enc, many_e)
        local(out_n, out_n, e_send.at[n]).wait()
    local(s_in.at[many_e], s_in.at[many_e], sc_sem.at[0]).wait()
    local(xcol.at[z, many_f], xcol.at[z, many_f], t_sem.at[0]).wait()
    local(m_all.at[many_f], m_all.at[many_f], m_sem.at[0]).wait()
    for h in range(2):
        for step in range(ups):
            local(cut(0, 0), cut(0, 0), zu_sem.at[0, h, step]).wait()
        for step in range(downs):
            local(cut(0, 0), cut(0, 0), zd_sem.at[0, h, step]).wait()
    local(m_col.at[many_z], m_col.at[many_z], zm_sem.at[0]).wait()
    for k in range(2):
        local(slots.at[k, many_x], slots.at[k, many_x], x_sem.at[0, k]).wait()
        for c in range(2):
            local(pa.at[k, c], pa.at[k, c], a_sem.at[0, k, c]).wait()
            for d in range(2 if ny == 4 else 1):
                local(rc.at[k, c, d], rc.at[k, c, d], b_sem.at[0, k, c, 2 + d]).wait()
                if ny == 4:
                    local(rl.at[k, c, d], rl.at[k, c, d], b_sem.at[0, k, c, d]).wait()
            local(hid.at[k, c, 0, many_y], hid.at[k, c, 0, many_y], h_sem.at[0, k, c]).wait()
            local(hid.at[k, c, 0], hid.at[k, c, 0], i_sem.at[0, k, c]).wait()
    for h in range(PIECES):
        for k in range(2):
            for c in range(2):
                local(orecv.at[h, k, c, many_x], orecv.at[h, k, c, many_x], o_sem.at[0, h, k, c]).wait()
        for step in range(ups):
            local(up_sum.at[h, 0], up_sum.at[h, 0], pu_sem.at[0, h, step]).wait()
        for step in range(downs):
            local(dn_sum.at[h, 0], dn_sum.at[h, 0], pd_sem.at[0, h, step]).wait()
        mine = fin.at[h, here]
        local(mine, mine, q_sem.at[2, h]).wait()
        rest = fin.at[h, many_f]
        local(rest, rest, q_sem.at[1, h]).wait()
        local(rest, rest, q_sem.at[0, h]).wait()


def run_layer(dims, rows, exps, tok, ids, probs):
    nz, nx, ny, fs, unit = dims
    ne, nf = nz * nx, 2 * ny
    gt, gs = nf * TOK, nf * CAP
    half, hidden, ups = nz * gs // 2, ne * unit, nz // 2
    chunk, hw, span = half // 2, fs // PIECES, unit * (fs // BLOCK)
    np = len(PARTS)
    vm = pl.BlockSpec(memory_space=pltpu.VMEM)
    hbm = pl.BlockSpec(memory_space=pltpu.HBM)
    anywhere = pl.BlockSpec(memory_space=pl.ANY)
    V = lambda *s: pltpu.VMEM(s, BF)
    W = lambda *s: pltpu.VMEM(s, F32)
    dma = lambda *s: pltpu.SemaphoreType.DMA(s)
    sums = [V(2, 2, ny, chunk, 2 * hidden)] * 4 + [V(2, 2, 2, chunk, 2 * hidden), V(2, 2, 2, chunk, hidden)]
    return pl.pallas_call(
        functools.partial(layer, dims),
        out_shape=(jax.ShapeDtypeStruct((2, 3, ne, unit, fs), BF), jax.ShapeDtypeStruct((TOK, nf * fs), BF)),
        in_specs=[hbm] * 5,
        out_specs=(vm, anywhere),
        scratch_shapes=[
            V(6, ne, unit, fs), pltpu.VMEM(exps.shape, jnp.int32), V(TOK, nf * fs), pltpu.VMEM(ids.shape, jnp.int32), W(*probs.shape), W(3, 2 * ne, span), W(3, 2 * ne, span), V(ne, 8, span), V(ne, 8, span),
            W(TOK, 128), W(PIECES, nz, gt, hw), V(nz, gt, fs), W(gt, 128), W(nz, 16, gt), W(nz, 16, gt),
            V(nx, 2, nz * gs, fs), V(2, nx, nz * gs, fs), V(2 * hidden, fs), V(PIECES, hidden, hw),
            *sums,
            V(2, 2, 2, ny, chunk, hidden), V(PIECES, 2, 2, nx, 2 * chunk, hw), V(PIECES, 2, 2, nx, 2 * chunk, hw),
            V(PIECES, 2, ups, gt, hw), V(PIECES, ups, gt, hw), V(PIECES, ups, gt, hw), V(PIECES, gt, hw),
            dma(6), dma(4), dma(np), dma(np), dma(np), dma(3), dma(3), dma(3), dma(2, 2, ups), dma(2, 2, ups), dma(3), dma(2, 2), dma(2),
            dma(2, 2, 2), dma(2, 2, 2, 4), dma(2, 2, 2), dma(2, 2, 2), dma(2, PIECES, 2, 2), dma(PIECES, 2, 2), dma(2, PIECES, ups), dma(2, PIECES, ups), dma(3, PIECES),
        ],
        compiler_params=pltpu.CompilerParams(collective_id=1, has_side_effects=True, vmem_limit_bytes=VMEM_LIMIT),
        name="layer",
    )(rows, exps, tok, ids, probs)


def body(dims, tokens, learner_rows, exponents, expert_ids, route_probs):
    nz, nx, ny, fs, unit = dims
    ne = nz * nx
    el, mixed = run_layer(dims, learner_rows.reshape(ne, 2, 3, unit, fs), exponents.transpose(1, 2, 3, 0), tokens, expert_ids.T, route_probs.T)
    return el.reshape(2, 3, ne * unit, fs), mixed


def make(mesh, dims):
    return jax.shard_map(
        functools.partial(body, dims),
        mesh=mesh,
        in_specs=(
            P(("fsdp", "expert"), None),
            P(None, None, "expert", "fsdp"),
            P(None, None, "expert", "fsdp"),
            P(("fsdp", "expert"), None),
            P(("fsdp", "expert"), None),
        ),
        out_specs=(P("expert", None, None, "fsdp"), P(("fsdp", "expert"), None)),
        check_vma=False,
    )


def solution(mesh):
    return make(mesh, (8, 4, 4, 512, 24))
```
